768 devices in a mesh: flow: 48 (over z, y_hi), chem: 16 (over x, y_lo, core).
Axes of the slice: x: 4, y: 8 (y_hi: 4, y_lo: 2; y = y_hi * 2 + y_lo), z: 12, core: 2. Of those that a mesh axis runs over, the one named last changes fastest.
Arguments:
- molar_fractions: float32 [53, 192, 112, 128], P(None, 'flow', 'chem'), may hold values from 0.05 to 2
- fluid_speed_vector: float32 [3, 192, 112, 128], P(None, 'flow', 'chem'), may hold values from -0.3 to 0.3
- thermal_state: float32 [192, 112, 128], P('flow', 'chem'), may hold values from 0.8 to 2
- molecular_spreading: float32 [53], replicated, may hold values from 0.05 to 0.12
- arrhenius_ln_amplitude: float32 [325], replicated, may hold values from -1 to 2
- arrhenius_energy: float32 [325], replicated, may hold values from 0.5 to 3
- consumed_molecules: int32 [325, 2], replicated, may hold values from 0 to 52
- resulting_molecules: int32 [325, 2], replicated, may hold values from 0 to 52
- patch_assignee: int32 [48, 224], P('flow'), may hold values from 0 to 16, as said below
Outputs:
- species_next: float32 [53, 192, 112, 128], P(None, 'flow', 'chem')
The draws below stay inside these ranges and needn't reach their ends.
Inputs may be any that keep to these rules, and one draw needn't show every extreme that they name: patch_assignee[f, b] names the chemistry index that handles block b of flow index f; the value 16 means that the block takes no chemistry. Exactly 112 blocks of every flow index take chemistry, and some box of every flow index has all its 14 blocks taking chemistry. At most 1 block of one box goes to one chemistry index, and at most 10 blocks of a flow index to one chemistry index; both bounds are reached in every flow index.
All inputs are finite; a program needn't handle non-finite values.
Results may differ from the reference program's by a relative error of at most 0.0003.
Values sent between devices are 32-bit elements; how exact they have to be, the bound alone decides.
No kernel may reach another device: no remote copies, remote signals or barrier semaphores. Data moves between devices by JAX's collectives and lax.ppermute only.
A program may use at most 32 MiB of HBM per device.

```python
import math
import jax
import jax.numpy as jnp
from jax import lax

S = 53
R = 325
SUBDOMAIN_WIDTH = 4
SUBDOMAIN_DEPTH = 7
SUBDOMAIN_HEIGHT = 128
PATCHES_ON_UNIT = 14
SUBSTEPS = 4
POINTS_IN_PATCH = 256
MESH_WIDTH = 192
MESH_DEPTH = 112
MESH_HEIGHT = 128
N_FLOW = 48
N_CHEM = 16


def draw_molar_fractions(key, part):
    key_rough = jax.random.fold_in(jax.random.fold_in(key, 11), 0)
    return jnp.exp(jax.random.uniform(key_rough, (S, MESH_WIDTH, MESH_DEPTH, MESH_HEIGHT), jnp.float32, math.log(0.05), math.log(2.0)))


def owner_group(key):
    kinetics_workers = N_CHEM
    patches = PATCHES_ON_UNIT
    patch_limit = max(1, -(-patches // (kinetics_workers - 1)))
    feeding_count = min(kinetics_workers, (patches * 3 // 4 + patch_limit - 1) // patch_limit)
    overall = kinetics_workers * patches
    key_busy, key_order, key_chosen, key_priority, key_shift = jax.random.split(key, 5)
    heaviest_loaded = jax.random.randint(key_busy, (), 0, kinetics_workers)
    shift_start = jax.random.randint(key_shift, (), 0, kinetics_workers - 1)
    order_src = jax.random.permutation(key_order, kinetics_workers)
    feeding = order_src < feeding_count
    flame_front = order_src == 0
    selected_patch = jax.random.randint(key_chosen, (kinetics_workers,), 0, patches // patch_limit)
    group_of = jnp.arange(patches, dtype=jnp.int32) // patch_limit
    to_busiest = feeding[:, None] & (group_of[None, :] == selected_patch[:, None])
    forced = to_busiest | flame_front[:, None]
    priority = jax.random.permutation(key_priority, overall).reshape(kinetics_workers, patches) + forced.astype(jnp.int32) * overall
    ranking = jnp.argsort(-priority.reshape(-1))
    placing = jnp.zeros((overall,), jnp.int32).at[ranking].set(jnp.arange(overall, dtype=jnp.int32))
    active = placing < overall // 2
    busy_flat = to_busiest.reshape(-1)
    remaining = active & jnp.logical_not(busy_flat)
    rest_rank = jnp.cumsum(remaining.astype(jnp.int32)) - 1
    others = (heaviest_loaded + 1 + (rest_rank + shift_start) % (kinetics_workers - 1)) % kinetics_workers
    destination = jnp.where(busy_flat, heaviest_loaded, others)
    return jnp.where(active, destination, kinetics_workers).astype(jnp.int32)


def draw_patch_assignee(key, part):
    subkeys = jax.random.split(jax.random.fold_in(key, 7), N_FLOW)
    return jax.vmap(owner_group)(subkeys)


def with_ends(result, stream_key, smallest, high):
    spot = [jax.random.randint(jax.random.fold_in(stream_key, axis), (), 0, length) for axis, length in enumerate(result.shape)]
    longest = result.shape.index(max(result.shape))
    neighbour = spot[:longest] + [(spot[longest] + 1) % result.shape[longest]] + spot[longest + 1:]
    return result.at[tuple(spot)].set(smallest).at[tuple(neighbour)].set(high)


def level_of(own_key, dims, pieces, smallest, largest):
    loudness = 1.0
    for position, shards_of in pieces:
        draws = jax.random.uniform(jax.random.fold_in(jax.random.fold_in(own_key, 6), position), (shards_of,), jnp.float32, smallest / len(pieces), largest / len(pieces))
        loudness = loudness * jnp.repeat(jnp.exp(draws), dims[position] // shards_of).reshape((-1,) + (1,) * (len(dims) - 1 - position))
    return loudness


def noise(stream_key, dims, spread, reach, cuts=(), held_as=jnp.bfloat16):
    values = jax.random.normal(stream_key, dims, jnp.float32) * spread
    if len(cuts) > 0:
        values = level_of(stream_key, dims, cuts, -0.22, 0.18) * values
    return jnp.clip(values, min=-reach, max=reach).astype(held_as)


def setup_inputs(seed: int = 0) -> dict:
    key_of = jax.random.split(jax.random.key(seed), 10)
    molar_fractions = draw_molar_fractions(jax.random.fold_in(key_of[9], 71), 0)
    fluid_speed_vector = noise(key_of[1], (3, MESH_WIDTH, MESH_DEPTH, MESH_HEIGHT), 0.1, 0.3, ((1, 48), (2, 16)), jnp.float32)
    thermal_state = jnp.clip(0.8 + 1.2 * jax.random.uniform(key_of[2], (MESH_WIDTH, MESH_DEPTH, MESH_HEIGHT), jnp.float32) ** level_of(key_of[2], (MESH_WIDTH, MESH_DEPTH, MESH_HEIGHT), ((0, 48), (1, 16)), -0.2, 0.2), 0.8, 2.0)
    molecular_spreading = jnp.clip(jnp.exp(jax.random.uniform(key_of[3], (S,), jnp.float32, math.log(0.05), math.log(0.12))), 0.05, 0.12)
    arrhenius_ln_amplitude = jnp.clip(jax.random.uniform(key_of[4], (R,), jnp.float32, -1.0, 2.0), -1.0, 2.0)
    arrhenius_energy = jnp.clip(jnp.exp(jax.random.uniform(key_of[5], (R,), jnp.float32, math.log(0.5), math.log(3.0))), 0.5, 3.0)
    consumed_molecules = with_ends(jax.random.randint(key_of[6], (R, 2), 0, S), jax.random.fold_in(key_of[6], 1), 0, S - 1).astype(jnp.int32)
    resulting_molecules = with_ends(jax.random.randint(key_of[7], (R, 2), 0, S), jax.random.fold_in(key_of[7], 1), 0, S - 1).astype(jnp.int32)
    patch_assignee = draw_patch_assignee(jax.random.fold_in(key_of[9], 71), 0)
    return {"molar_fractions": molar_fractions, "fluid_speed_vector": fluid_speed_vector, "thermal_state": thermal_state, "molecular_spreading": molecular_spreading, "arrhenius_ln_amplitude": arrhenius_ln_amplitude, "arrhenius_energy": arrhenius_energy, "consumed_molecules": consumed_molecules, "resulting_molecules": resulting_molecules, "patch_assignee": patch_assignee}


conc_floor = 0.1
rate_ceiling = 1.0
chem_dt = 0.04


def derivatives(neighbours):
    minus_two, minus_one, center, plus_one, plus_two = neighbours
    first = (minus_two - 8.0 * minus_one + 8.0 * plus_one - plus_two) / 12.0
    second = (-minus_two + 16.0 * minus_one - 30.0 * center + 16.0 * plus_one - plus_two) / 12.0
    return first, second


def rolled(values, which_axis):
    return derivatives((jnp.roll(values, 2, which_axis), jnp.roll(values, 1, which_axis), values, jnp.roll(values, -1, which_axis), jnp.roll(values, -2, which_axis)))


def stoichiometry(consumed_molecules, resulting_molecules, species_count):
    species_ids = jnp.arange(species_count, dtype=jnp.int32)
    forward = (consumed_molecules[:, 0:1] == species_ids[None, :]).astype(jnp.float32) + (consumed_molecules[:, 1:2] == species_ids[None, :]).astype(jnp.float32)
    produced = (resulting_molecules[:, 0:1] == species_ids[None, :]).astype(jnp.float32) + (resulting_molecules[:, 1:2] == species_ids[None, :]).astype(jnp.float32)
    return forward, (produced - forward).T


def react(initial, kelvin, forward, net_change, arrhenius_ln_amplitude, arrhenius_energy):
    current = initial
    for substep in range(SUBSTEPS):
        logged = jnp.log(jnp.maximum(current, conc_floor))
        exponent = arrhenius_ln_amplitude[:, None] + jnp.dot(forward, logged, preferred_element_type=jnp.float32, precision=lax.Precision.HIGHEST) - arrhenius_energy[:, None] / kelvin[None, :]
        progress = jnp.exp(jnp.minimum(exponent, rate_ceiling))
        current = current + chem_dt * jnp.dot(net_change, progress, preferred_element_type=jnp.float32, precision=lax.Precision.HIGHEST)
    return current - initial


def reference(molar_fractions, fluid_speed_vector, thermal_state, molecular_spreading, arrhenius_ln_amplitude, arrhenius_energy, consumed_molecules, resulting_molecules, patch_assignee):
    def advance(packed):
        values, coefficient = packed
        first_x, second_x = rolled(values, 0)
        first_y, second_y = rolled(values, 1)
        first_z, second_z = rolled(values, 2)
        moved = fluid_speed_vector[0] * first_x + fluid_speed_vector[1] * first_y + fluid_speed_vector[2] * first_z
        return values - moved + coefficient * (second_x + second_y + second_z)

    advected = lax.map(advance, (molar_fractions, molecular_spreading))
    forward, net_change = stoichiometry(consumed_molecules, resulting_molecules, S)
    half_count = N_CHEM * PATCHES_ON_UNIT // 2
    patches = advected.reshape(S, N_FLOW, SUBDOMAIN_WIDTH, N_CHEM, SUBDOMAIN_DEPTH, SUBDOMAIN_HEIGHT).transpose(1, 3, 0, 2, 4, 5)
    patches = patches.reshape(N_FLOW, N_CHEM, S, PATCHES_ON_UNIT, POINTS_IN_PATCH).transpose(0, 1, 3, 2, 4).reshape(N_FLOW, N_CHEM * PATCHES_ON_UNIT, S, POINTS_IN_PATCH)
    patch_enthalpy_output = thermal_state.reshape(N_FLOW, SUBDOMAIN_WIDTH, N_CHEM, SUBDOMAIN_DEPTH, SUBDOMAIN_HEIGHT).transpose(0, 2, 1, 3, 4).reshape(N_FLOW, N_CHEM * PATCHES_ON_UNIT, POINTS_IN_PATCH)

    def per_group(packed):
        group_blocks, group_heat, group_owner = packed
        active = group_owner < N_CHEM
        selected_patch = jnp.argsort(jnp.where(active, 0, 1).astype(jnp.int32), stable=True)[:half_count]
        picked = group_blocks[selected_patch].transpose(1, 0, 2).reshape(S, half_count * POINTS_IN_PATCH)
        kelvin = group_heat[selected_patch].reshape(half_count * POINTS_IN_PATCH)
        source = react(picked, kelvin, forward, net_change, arrhenius_ln_amplitude, arrhenius_energy)
        source = source.reshape(S, half_count, POINTS_IN_PATCH).transpose(1, 0, 2)
        return group_blocks + jnp.zeros_like(group_blocks).at[selected_patch].set(source)

    updated = lax.map(per_group, (patches, patch_enthalpy_output, patch_assignee))
    updated = updated.reshape(N_FLOW, N_CHEM, PATCHES_ON_UNIT, S, POINTS_IN_PATCH).transpose(0, 1, 3, 2, 4).reshape(N_FLOW, N_CHEM, S, SUBDOMAIN_WIDTH, SUBDOMAIN_DEPTH, SUBDOMAIN_HEIGHT)
    return updated.transpose(2, 0, 3, 1, 4, 5).reshape(S, N_FLOW * SUBDOMAIN_WIDTH, N_CHEM * SUBDOMAIN_DEPTH, SUBDOMAIN_HEIGHT)
```

```python
import jax
import jax.numpy as jnp
from jax import lax
from jax.experimental import pallas as pl
from jax.experimental.pallas import tpu as pltpu
from jax.sharding import PartitionSpec as P

PATCHES_ON_UNIT = 14
SUBSTEPS = 4
LOG2E = 1.4426950408889634
CONC_FLOOR = 0.1
CHEM_DT = 0.04
ROWS = 64
LANES = 128


def ring(axis):
    count = lax.axis_size(axis)
    forward = [(i, (i + 1) % count) for i in range(count)]
    return forward, [(target, source) for source, target in forward]


def pieces(values):
    high = lax.reduce_precision(values, 8, 7)
    middle = lax.reduce_precision(values - high, 8, 7)
    return high, middle, values - high - middle


def tables(consumed, resulting, ln_amplitude, energy, species):
    count = consumed.shape[0]
    padded = -(-count // 16) * 16
    ids = jnp.arange(ROWS, dtype=jnp.int32)
    used = (consumed[:, 0:1] == ids).astype(jnp.float32) + (consumed[:, 1:2] == ids).astype(jnp.float32)
    a_high, a_middle, a_low = pieces(ln_amplitude * LOG2E)
    e_high, e_middle, e_low = pieces(energy * -LOG2E)
    spare = jnp.stack([a_high, e_high, a_middle, a_low, e_middle, e_low], axis=1)
    spare = jnp.pad(spare, ((0, 0), (species, ROWS - species - 6)))
    gather = jnp.concatenate([used + spare, used + spare], axis=1)
    gather = jnp.pad(gather, ((0, padded - count), (0, 0))).astype(jnp.bfloat16)
    takes = consumed.T
    gives = resulting.T
    change = (
        (gives[0:1] == ids[:, None]).astype(jnp.float32)
        + (gives[1:2] == ids[:, None]).astype(jnp.float32)
        - (takes[0:1] == ids[:, None]).astype(jnp.float32)
        - (takes[1:2] == ids[:, None]).astype(jnp.float32)
    )
    change = jnp.pad(change, ((0, 0), (0, padded - count)))
    return gather, jnp.concatenate([change, change], axis=1).astype(jnp.bfloat16)


def split(values):
    high = values.astype(jnp.bfloat16)
    low = (values - high.astype(jnp.float32)).astype(jnp.bfloat16)
    return jnp.concatenate([high, low], axis=0)


def step_kernel(
    u_ref, xlo_ref, xhi_ref, ylo_ref, yhi_ref, field_ref, spread_ref, gather_ref, change_ref, out_ref, wide_ref
):
    species, depth, width, lanes = u_ref.shape
    stride = depth + 4
    slab = wide_ref.shape[1]

    def fill(ref, y_offset, x_offset):
        _, ys, xs, _ = ref.shape
        flat = ref.reshape(species * ys * xs, lanes)
        for y in range(ys):
            for x in range(xs):
                wide_ref[(x + x_offset) * stride + y + y_offset, 0:species, :] = flat[
                    pl.ds(y * xs + x, species, stride=ys * xs), :
                ]

    fill(u_ref, 2, 2)
    fill(xlo_ref, 2, 0)
    fill(xhi_ref, 2, width + 2)
    fill(ylo_ref, 0, 2)
    fill(yhi_ref, depth + 2, 2)

    out_flat = out_ref.reshape(species * depth * width, lanes)
    spread = spread_ref[...] * (1.0 / 12.0)

    def advect(row, field):
        x = row // depth
        y = row - x * depth
        base = (x + 2) * stride + y + 2
        center = wide_ref[base]
        near = jnp.zeros_like(center)
        far = jnp.zeros_like(center)
        moved = jnp.zeros_like(center)
        for axis in range(3):
            if axis == 2:
                low2 = pltpu.roll(center, 2, 1)
                low1 = pltpu.roll(center, 1, 1)
                high1 = pltpu.roll(center, lanes - 1, 1)
                high2 = pltpu.roll(center, lanes - 2, 1)
            else:
                hop = stride if axis == 0 else 1
                low2 = wide_ref[base - 2 * hop]
                low1 = wide_ref[base - hop]
                high1 = wide_ref[base + hop]
                high2 = wide_ref[base + 2 * hop]
            speed = field[axis : axis + 1] * (1.0 / 12.0)
            moved = moved + speed * (8.0 * (high1 - low1) - (high2 - low2))
            near = near + (high1 + low1)
            far = far + (high2 + low2)
        return center - moved + spread * (16.0 * near - far - 90.0 * center)

    row_ids = lax.broadcasted_iota(jnp.int32, (16, 2 * lanes), 0) + (ROWS - 16)
    is_species = row_ids < species
    is_one = (row_ids == species) | (row_ids == species + 2) | (row_ids == species + 3)
    is_heat = (row_ids == species + 1) | (row_ids == species + 4) | (row_ids == species + 5)

    def block(b, carry):
        field = field_ref[b]
        advected = jnp.concatenate(
            [advect(2 * b + k, field[:, k * lanes : (k + 1) * lanes]) for k in range(2)], axis=1
        )
        advected = jnp.concatenate(
            [advected, jnp.zeros((ROWS - slab, 2 * lanes), jnp.float32)], axis=0
        )
        spare = jnp.where(is_one, 1.0, jnp.where(is_heat, field[3:4], 0.0))
        current = advected
        for _ in range(SUBSTEPS):
            logged = jnp.log(jnp.maximum(current, CONC_FLOOR)) * LOG2E
            stacked = jnp.concatenate(
                [logged[: ROWS - 16], jnp.where(is_species, logged[ROWS - 16 :], spare)], axis=0
            )
            exponent = jnp.dot(gather_ref[...], split(stacked), preferred_element_type=jnp.float32)
            progress = jnp.exp2(jnp.minimum(exponent, LOG2E))
            current = current + CHEM_DT * jnp.dot(
                change_ref[...], split(progress), preferred_element_type=jnp.float32
            )
        result = jnp.where(field[4:5] > 0.5, current, advected)
        for k in range(2):
            row = 2 * b + k
            x = row // depth
            y = row - x * depth
            out_flat[pl.ds(y * width + x, species, stride=depth * width), :] = result[
                0:species, k * lanes : (k + 1) * lanes
            ]
        return carry

    lax.fori_loop(0, PATCHES_ON_UNIT, block, 0)


def per_device(
    molar_fractions,
    fluid_speed_vector,
    thermal_state,
    molecular_spreading,
    arrhenius_ln_amplitude,
    arrhenius_energy,
    consumed_molecules,
    resulting_molecules,
    patch_assignee,
):
    species, width, depth, lanes = molar_fractions.shape
    cells = molar_fractions.transpose(0, 2, 1, 3)
    flow_next, flow_back = ring("flow")
    chem_next, chem_back = ring("chem")
    xlo = lax.ppermute(cells[:, :, width - 2 :], "flow", flow_next)
    xhi = lax.ppermute(cells[:, :, :2], "flow", flow_back)
    ylo = lax.ppermute(cells[:, depth - 2 :], "chem", chem_next)
    yhi = lax.ppermute(cells[:, :2], "chem", chem_back)

    gather, change = tables(
        consumed_molecules, resulting_molecules, arrhenius_ln_amplitude, arrhenius_energy, species
    )
    workers = lax.axis_size("chem")
    owners = lax.dynamic_slice_in_dim(
        patch_assignee[0], lax.axis_index("chem") * PATCHES_ON_UNIT, PATCHES_ON_UNIT
    )
    active = (owners < workers).astype(jnp.float32)
    points = width * depth * lanes // PATCHES_ON_UNIT
    field = jnp.concatenate(
        [
            fluid_speed_vector.reshape(3, PATCHES_ON_UNIT, points),
            (1.0 / thermal_state).reshape(1, PATCHES_ON_UNIT, points),
            jnp.broadcast_to(active[None, :, None], (1, PATCHES_ON_UNIT, points)),
            jnp.zeros((3, PATCHES_ON_UNIT, points), jnp.float32),
        ],
        axis=0,
    ).transpose(1, 0, 2)
    slab = -(-species // 8) * 8
    spread = jnp.broadcast_to(
        jnp.pad(molecular_spreading, (0, slab - species))[:, None], (slab, LANES)
    )
    out = pl.pallas_call(
        step_kernel,
        out_shape=jax.ShapeDtypeStruct(cells.shape, jnp.float32),
        scratch_shapes=[pltpu.VMEM(((width + 4) * (depth + 4), slab, lanes), jnp.float32)],
        name="step",
    )(cells, xlo, xhi, ylo, yhi, field, spread, gather, change)
    return out.transpose(0, 2, 1, 3)


def solution(mesh):
    in_specs = (
        P(None, "flow", "chem", None),
        P(None, "flow", "chem", None),
        P("flow", "chem", None),
        P(),
        P(),
        P(),
        P(),
        P(),
        P("flow", None),
    )
    out_specs = P(None, "flow", "chem", None)
    return jax.shard_map(
        per_device, mesh=mesh, in_specs=in_specs, out_specs=out_specs, check_vma=False
    )
```

```python
import functools

import jax
import jax.numpy as jnp
from jax import lax
from jax.experimental import pallas as pl
from jax.experimental.pallas import tpu as pltpu
from jax.sharding import PartitionSpec as P

PATCHES_ON_UNIT = 14
SUBSTEPS = 4
LOG2E = 1.4426950408889634
CONC_FLOOR = 0.1
CHEM_DT = 0.04
ROWS = 64
CHUNKS = 3


def ring(axis):
    count = lax.axis_size(axis)
    forward = [(i, (i + 1) % count) for i in range(count)]
    return forward, [(target, source) for source, target in forward]


def pieces(values):
    high = lax.reduce_precision(values, 8, 7)
    middle = lax.reduce_precision(values - high, 8, 7)
    return high, middle, values - high - middle


def tables(consumed, resulting, ln_amplitude, energy, species):
    count = consumed.shape[0]
    step = 16 * CHUNKS
    padded = -(-count // step) * step
    ids = jnp.arange(ROWS, dtype=jnp.int32)
    used = (consumed[:, 0:1] == ids).astype(jnp.float32) + (consumed[:, 1:2] == ids).astype(jnp.float32)
    a_high, a_middle, a_low = pieces(ln_amplitude * LOG2E)
    e_high, e_middle, e_low = pieces(energy * -LOG2E)
    spare = jnp.stack([a_high, e_high, a_middle, a_low, e_middle, e_low], axis=1)
    spare = jnp.pad(spare, ((0, 0), (species, ROWS - species - 6)))
    gather = jnp.concatenate([used + spare, used + spare], axis=1)
    gather = jnp.pad(gather, ((0, padded - count), (0, 0))).astype(jnp.bfloat16)
    takes = consumed.T
    gives = resulting.T
    change = (
        (gives[0:1] == ids[:, None]).astype(jnp.float32)
        + (gives[1:2] == ids[:, None]).astype(jnp.float32)
        - (takes[0:1] == ids[:, None]).astype(jnp.float32)
        - (takes[1:2] == ids[:, None]).astype(jnp.float32)
    )
    change = jnp.pad(change, ((0, 0), (0, padded - count)))
    change = change.reshape(ROWS, CHUNKS, padded // CHUNKS).transpose(1, 0, 2)
    return gather, jnp.concatenate([change, change], axis=2).astype(jnp.bfloat16)


def split(values):
    high = values.astype(jnp.bfloat16)
    low = (values - high.astype(jnp.float32)).astype(jnp.bfloat16)
    return jnp.concatenate([high, low], axis=0)


def half_kernel(first_x, *refs):
    u_ref, side_ref, ylo_ref, yhi_ref, field_ref, spread_ref, gather_ref, change_ref = refs[:8]
    out_ref, wide_ref, advected_ref, current_ref = refs[-4:]
    species, depth, width, lanes = u_ref.shape
    tiles = field_ref.shape[0]
    stride = depth + 4
    slab = wide_ref.shape[1]

    def fill(ref, ys, xs, y_offset, slot):
        _, all_y, all_x, _ = ref.shape
        flat = ref.reshape(species * all_y * all_x, lanes)
        for y in ys:
            for k, x in enumerate(xs):
                wide_ref[(slot + k) * stride + y + y_offset, 0:species, :] = flat[
                    pl.ds(y * all_x + x, species, stride=all_y * all_x), :
                ]

    fill(u_ref, range(depth), range(width), 2, 2 - first_x)
    fill(side_ref, range(depth), range(2), 2, 0 if first_x == 0 else 4)
    fill(ylo_ref, range(2), (first_x, first_x + 1), 0, 2)
    fill(yhi_ref, range(2), (first_x, first_x + 1), depth + 2, 2)
    spread = spread_ref[...] * (1.0 / 12.0)

    def advect(row, field):
        x = row // depth
        y = row - x * depth
        base = (x + 2) * stride + y + 2
        center = wide_ref[base]
        near = jnp.zeros_like(center)
        far = jnp.zeros_like(center)
        moved = jnp.zeros_like(center)
        for axis in range(3):
            if axis == 2:
                low2 = pltpu.roll(center, 2, 1)
                low1 = pltpu.roll(center, 1, 1)
                high1 = pltpu.roll(center, lanes - 1, 1)
                high2 = pltpu.roll(center, lanes - 2, 1)
            else:
                hop = stride if axis == 0 else 1
                low2 = wide_ref[base - 2 * hop]
                low1 = wide_ref[base - hop]
                high1 = wide_ref[base + hop]
                high2 = wide_ref[base + 2 * hop]
            speed = field[axis : axis + 1] * (1.0 / 12.0)
            moved = moved + speed * (8.0 * (high1 - low1) - (high2 - low2))
            near = near + (high1 + low1)
            far = far + (high2 + low2)
        return center - moved + spread * (16.0 * near - far - 90.0 * center)

    def advect_tile(t, carry):
        for k in range(2):
            part = slice(k * lanes, (k + 1) * lanes)
            advected = advect(2 * t + k, field_ref[t, :, part])
            current_ref[t, 0:slab, part] = advected
            advected_ref[t, 0:slab, part] = advected
        current_ref[t, slab:ROWS] = jnp.zeros((ROWS - slab, 2 * lanes), jnp.float32)
        return carry

    lax.fori_loop(0, tiles, advect_tile, 0)

    row_ids = lax.broadcasted_iota(jnp.int32, (16, 2 * lanes), 0) + (ROWS - 16)
    is_species = row_ids < species
    is_one = (row_ids == species) | (row_ids == species + 2) | (row_ids == species + 3)
    is_heat = (row_ids == species + 1) | (row_ids == species + 4) | (row_ids == species + 5)

    def exponent(t):
        logged = jnp.log(jnp.maximum(current_ref[t], CONC_FLOOR)) * LOG2E
        spare = jnp.where(is_one, 1.0, jnp.where(is_heat, field_ref[t, 3:4], 0.0))
        stacked = jnp.concatenate(
            [logged[: ROWS - 16], jnp.where(is_species, logged[ROWS - 16 :], spare)], axis=0
        )
        return jnp.dot(gather_ref[...], split(stacked), preferred_element_type=jnp.float32)

    size = gather_ref.shape[0] // CHUNKS

    def gained(powers):
        total = None
        for j in range(CHUNKS):
            progress = jnp.exp2(jnp.minimum(powers[j * size : (j + 1) * size], LOG2E))
            part = jnp.dot(change_ref[j], split(progress), preferred_element_type=jnp.float32)
            total = part if total is None else total + part
        return CHEM_DT * total

    def substep(i, carry):
        ready = exponent(0)
        for t in range(tiles):
            powers = ready
            if t + 1 < tiles:
                ready = exponent(t + 1)
            current_ref[t] = current_ref[t] + gained(powers)
        return carry

    lax.fori_loop(0, SUBSTEPS, substep, 0)

    for t in range(tiles):
        result = jnp.where(field_ref[t, 4:5] > 0.5, current_ref[t], advected_ref[t])
        if first_x != 0:
            out_ref[t] = result
            continue
        out_flat = out_ref.reshape(species * depth * width, lanes)
        for values, shift in ((result, 0), (refs[8][t], 2)):
            for k in range(2):
                x, y = divmod(2 * t + k, depth)
                out_flat[pl.ds(y * width + x + shift, species, stride=depth * width), :] = values[
                    0:species, k * lanes : (k + 1) * lanes
                ]


def half(first_x, cells, side, ylo, yhi, field, spread, gather, change, *other):
    _, depth, _, lanes = cells.shape
    tiles = field.shape[0]
    block = (tiles, ROWS, 2 * lanes)
    shape = block if first_x else cells.shape
    return pl.pallas_call(
        functools.partial(half_kernel, first_x),
        out_shape=jax.ShapeDtypeStruct(shape, jnp.float32),
        scratch_shapes=[
            pltpu.VMEM((6 * (depth + 4), spread.shape[0], lanes), jnp.float32),
            pltpu.VMEM(block, jnp.float32),
            pltpu.VMEM(block, jnp.float32),
        ],
    )(cells, side, ylo, yhi, field, spread, gather, change, *other)


def per_device(
    molar_fractions,
    fluid_speed_vector,
    thermal_state,
    molecular_spreading,
    arrhenius_ln_amplitude,
    arrhenius_energy,
    consumed_molecules,
    resulting_molecules,
    patch_assignee,
):
    species, width, depth, lanes = molar_fractions.shape
    cells = molar_fractions.transpose(0, 2, 1, 3)
    flow_next, flow_back = ring("flow")
    chem_next, chem_back = ring("chem")
    xlo = lax.ppermute(cells[:, :, width - 2 :], "flow", flow_next)
    xhi = lax.ppermute(cells[:, :, :2], "flow", flow_back)
    ylo = lax.ppermute(cells[:, depth - 2 :], "chem", chem_next)
    yhi = lax.ppermute(cells[:, :2], "chem", chem_back)

    gather, change = tables(
        consumed_molecules, resulting_molecules, arrhenius_ln_amplitude, arrhenius_energy, species
    )
    workers = lax.axis_size("chem")
    owners = lax.dynamic_slice_in_dim(
        patch_assignee[0], lax.axis_index("chem") * PATCHES_ON_UNIT, PATCHES_ON_UNIT
    )
    active = (owners < workers).astype(jnp.float32)
    points = width * depth * lanes // PATCHES_ON_UNIT
    field = jnp.concatenate(
        [
            fluid_speed_vector.reshape(3, PATCHES_ON_UNIT, points),
            (1.0 / thermal_state).reshape(1, PATCHES_ON_UNIT, points),
            jnp.broadcast_to(active[None, :, None], (1, PATCHES_ON_UNIT, points)),
            jnp.zeros((3, PATCHES_ON_UNIT, points), jnp.float32),
        ],
        axis=0,
    ).transpose(1, 0, 2)
    slab = -(-species // 8) * 8
    spread = jnp.broadcast_to(
        jnp.pad(molecular_spreading, (0, slab - species))[:, None], (slab, lanes)
    )
    middle = PATCHES_ON_UNIT // 2
    upper = half(2, cells, xhi, ylo, yhi, field[middle:], spread, gather, change)
    out = half(0, cells, xlo, ylo, yhi, field[:middle], spread, gather, change, upper)
    return out.transpose(0, 2, 1, 3)


def solution(mesh):
    in_specs = (
        P(None, "flow", "chem", None),
        P(None, "flow", "chem", None),
        P("flow", "chem", None),
        P(),
        P(),
        P(),
        P(),
        P(),
        P("flow", None),
    )
    out_specs = P(None, "flow", "chem", None)
    return jax.shard_map(
        per_device, mesh=mesh, in_specs=in_specs, out_specs=out_specs, check_vma=False
    )
```

```python
import functools

import jax
import jax.numpy as jnp
from jax import lax
from jax.experimental import pallas as pl
from jax.experimental.pallas import tpu as pltpu
from jax.sharding import PartitionSpec as P

PATCHES_ON_UNIT = 14
SUBSTEPS = 4
LOG2E = 1.4426950408889634
CONC_FLOOR = 0.1
CHEM_DT = 0.04
ROWS = 64
CHUNK = 128
UNROLL = 4


def ring(axis):
    count = lax.axis_size(axis)
    forward = [(i, (i + 1) % count) for i in range(count)]
    return forward, [(target, source) for source, target in forward]


def chunks(count):
    padded = -(-count // 16) * 16
    return [(start, min(CHUNK, padded - start)) for start in range(0, padded, CHUNK)]


def split(values):
    high = values.astype(jnp.bfloat16)
    low = (values - high.astype(jnp.float32)).astype(jnp.bfloat16)
    return jnp.concatenate([high, low], axis=0)


def pieces(values):
    high = values.astype(jnp.bfloat16).astype(jnp.float32)
    middle = (values - high).astype(jnp.bfloat16).astype(jnp.float32)
    return high, middle, values - high - middle


def strided(ref):
    species, ys, xs, lanes = ref.shape
    flat = ref.reshape(species * ys * xs, lanes)
    return lambda y, x: flat.at[pl.ds(y * xs + x, species, stride=ys * xs), :]


def prepare_kernel(
    u_ref, speed_ref, heat_ref, spread_ref, amplitude_ref, energy_ref, consumed_ref, resulting_ref,
    gather_ref, change_ref, field_ref, slow_ref, lower_ref, upper_ref, wide_ref, index_ref, rate_ref
):
    species, depth, width, lanes = u_ref.shape
    count = consumed_ref.shape[1]
    reach = index_ref.shape[1]
    slab = wide_ref.shape[1]
    stride = depth + 4

    index_ref[...] = jnp.full(index_ref.shape, -1, jnp.int32)
    index_ref[0:2, 0:count] = consumed_ref[...]
    index_ref[2:4, 0:count] = resulting_ref[...]
    rate_ref[...] = jnp.zeros_like(rate_ref)
    rate_ref[0:1, 0:count] = amplitude_ref[...] * LOG2E
    rate_ref[1:2, 0:count] = energy_ref[...] * -LOG2E
    ids = lax.broadcasted_iota(jnp.int32, (ROWS, reach), 0)
    ones = [jnp.where(index_ref[k : k + 1] == ids, 1.0, 0.0) for k in range(4)]
    used = ones[0] + ones[1]
    change = ones[2] + ones[3] - used
    a_high, a_middle, a_low = pieces(rate_ref[0:1])
    e_high, e_middle, e_low = pieces(rate_ref[1:2])
    for k, row in enumerate((a_high, e_high, a_middle, a_low, e_middle, e_low)):
        used = jnp.where(ids == species + k, row, used)
    both = jnp.concatenate([used, used], axis=0)
    rows = gather_ref.shape[0]
    for start in range(0, reach, lanes):
        size = min(lanes, rows - start)
        part = jnp.transpose(both[:, start : start + lanes])
        gather_ref[start : start + size] = part[0:size].astype(jnp.bfloat16)
    lane = lax.broadcasted_iota(jnp.int32, (ROWS, 2 * CHUNK), 1)
    for j, (start, size) in enumerate(chunks(count)):
        part = change[:, start : start + CHUNK]
        pair = jnp.concatenate([part, jnp.zeros_like(part)], axis=1)
        pair = jnp.where(lane < size, pair, 0.0)
        change_ref[j] = (pair + pltpu.roll(pair, size, 1)).astype(jnp.bfloat16)

    half = width // 2 * depth // 2
    for x in range(width):
        for y in range(depth):
            t, k = divmod(x * depth + y, 2)
            part = slice(k * lanes, (k + 1) * lanes)
            for c in range(3):
                field_ref[t, c : c + 1, part] = speed_ref[c, y, x : x + 1, :] * (1.0 / 12.0)
            field_ref[t, 3:4, part] = 1.0 / heat_ref[y, x : x + 1, :]
    spread = jnp.concatenate([spread_ref[...], jnp.zeros((1, lanes - species), jnp.float32)], axis=1)
    spread = jnp.transpose(jnp.broadcast_to(spread * (1.0 / 12.0), (lanes, lanes)))[0:slab]
    slow_ref[...] = spread

    for slot in range(width + 4):
        for y in range(stride):
            if 2 <= slot < width + 2 and 2 <= y < depth + 2:
                wide_ref[slot * stride + y, 0:species, :] = strided(u_ref)(y - 2, slot - 2)[...]
            elif 2 <= slot < width + 2 or 2 <= y < depth + 2:
                wide_ref[slot * stride + y] = jnp.zeros((slab, lanes), jnp.float32)

    def advect(row, field):
        x = row // depth
        y = row - x * depth
        base = (x + 2) * stride + y + 2
        center = wide_ref[base]
        near = jnp.zeros_like(center)
        far = jnp.zeros_like(center)
        moved = jnp.zeros_like(center)
        for axis in range(3):
            if axis == 2:
                low2 = pltpu.roll(center, 2, 1)
                low1 = pltpu.roll(center, 1, 1)
                high1 = pltpu.roll(center, lanes - 1, 1)
                high2 = pltpu.roll(center, lanes - 2, 1)
            else:
                hop = stride if axis == 0 else 1
                low2 = wide_ref[base - 2 * hop]
                low1 = wide_ref[base - hop]
                high1 = wide_ref[base + hop]
                high2 = wide_ref[base + 2 * hop]
            moved = moved + field[axis : axis + 1] * (8.0 * (high1 - low1) - (high2 - low2))
            near = near + (high1 + low1)
            far = far + (high2 + low2)
        return center - moved + spread * (16.0 * near - far - 90.0 * center)

    for target, shift in ((lower_ref, 0), (upper_ref, half)):
        def tile(t, carry, target=target, shift=shift):
            for k in range(2):
                part = slice(k * lanes, (k + 1) * lanes)
                target[t, 0:slab, part] = advect(2 * (t + shift) + k, field_ref[t + shift, :, part])
            target[t, slab:ROWS] = jnp.zeros((ROWS - slab, 2 * lanes), jnp.float32)
            return carry

        lax.fori_loop(0, half, tile, 0)


def prepare(cells, speed, heat, spread, amplitude, energy, consumed, resulting):
    species, depth, width, lanes = cells.shape
    count = consumed.shape[1]
    parts = chunks(count)
    reach = len(parts) * CHUNK
    slab = -(-species // 8) * 8
    tiles = width * depth // 2
    shapes = [
        ((parts[-1][0] + parts[-1][1], 2 * ROWS), jnp.bfloat16),
        ((len(parts), ROWS, 2 * CHUNK), jnp.bfloat16),
        ((tiles, 8, 2 * lanes), jnp.float32),
        ((slab, lanes), jnp.float32),
        ((tiles // 2, ROWS, 2 * lanes), jnp.float32),
        ((tiles // 2, ROWS, 2 * lanes), jnp.float32),
    ]
    return pl.pallas_call(
        prepare_kernel,
        out_shape=[jax.ShapeDtypeStruct(*shape) for shape in shapes],
        scratch_shapes=[
            pltpu.VMEM(((width + 4) * (depth + 4), slab, lanes), jnp.float32),
            pltpu.VMEM((8, reach), jnp.int32),
            pltpu.VMEM((8, reach), jnp.float32),
        ],
        name="prepare",
    )(cells, speed, heat, spread, amplitude, energy, consumed, resulting)


def half_kernel(first_x, workers, *refs):
    place_ref, owner_ref, base_ref, side_ref, ylo_ref, yhi_ref, field_ref, spread_ref = refs[:8]
    gather_ref, change_ref = refs[8:10]
    out_ref, advected_ref, current_ref = refs[-3:]
    species, depth, _, lanes = side_ref.shape
    tiles = base_ref.shape[0]
    first_tile = first_x * depth // 2
    side, ylo, yhi = strided(side_ref), strided(ylo_ref), strided(yhi_ref)
    spread = spread_ref[0:species]

    for t in range(tiles):
        for k in range(2):
            x, y = divmod(2 * t + k, depth)
            part = slice(k * lanes, (k + 1) * lanes)
            field = field_ref[first_tile + t, :, part]
            values = base_ref[t, 0:species, part]

            def add(values, axis, far, value):
                speed = field[axis : axis + 1]
                if far > 0:
                    speed = -speed
                return values + (speed * 8.0 + spread * 16.0 if abs(far) == 1 else -speed - spread) * value

            if first_x == 0:
                taps = ((-2, 0), (-1, 1)) if x == 0 else ((-2, 1),)
            else:
                taps = ((2, 0),) if x == 0 else ((1, 0), (2, 1))
            for far, plane in taps:
                values = add(values, 0, far, side(y, plane)[...])
            column = first_x + x
            if y == 0:
                values = add(values, 1, -2, ylo(0, column)[...])
            if y <= 1:
                values = add(values, 1, -1 - y, ylo(1, column)[...])
            if y >= depth - 2:
                values = add(values, 1, depth - y, yhi(0, column)[...])
            if y == depth - 1:
                values = add(values, 1, 2, yhi(1, column)[...])
            advected_ref[t, 0:species, part] = values
            current_ref[t, 0:species, part] = values
        current_ref[t, species:ROWS] = jnp.ones((ROWS - species, 2 * lanes), jnp.float32)

    row_ids = lax.broadcasted_iota(jnp.int32, (16, 2 * lanes), 0) + (ROWS - 16)
    is_species = row_ids < species
    is_one = (row_ids == species) | (row_ids == species + 2) | (row_ids == species + 3)
    is_heat = (row_ids == species + 1) | (row_ids == species + 4) | (row_ids == species + 5)

    def exponent(t):
        logged = jnp.log(jnp.maximum(current_ref[t], CONC_FLOOR)) * LOG2E
        spare = jnp.where(is_one, 1.0, jnp.where(is_heat, field_ref[first_tile + t, 3:4], 0.0))
        stacked = jnp.concatenate(
            [logged[: ROWS - 16], jnp.where(is_species, logged[ROWS - 16 :], spare)], axis=0
        )
        return jnp.dot(gather_ref[...], split(stacked), preferred_element_type=jnp.float32)

    def gained(powers):
        total = None
        for j, (start, size) in enumerate(chunks(powers.shape[0])):
            progress = jnp.exp2(jnp.minimum(powers[start : start + size], LOG2E))
            part = jnp.dot(
                change_ref[j, :, 0 : 2 * size], split(progress), preferred_element_type=jnp.float32
            )
            total = part if total is None else total + part
        return CHEM_DT * total

    def substeps(turns):
        order = [(i, t) for i in range(turns) for t in range(tiles)]
        ready = exponent(0)
        for n, (_, t) in enumerate(order):
            powers = ready
            if n + 1 < len(order):
                ready = exponent(order[n + 1][1])
            current_ref[t] = current_ref[t] + gained(powers)

    if UNROLL == SUBSTEPS:
        substeps(SUBSTEPS)
    else:
        def turn(i, carry):
            substeps(UNROLL)
            return carry

        lax.fori_loop(0, SUBSTEPS // UNROLL, turn, 0)

    for t in range(tiles):
        reacts = owner_ref[0, place_ref[0] * PATCHES_ON_UNIT + first_tile + t] < workers
        result = jnp.where(reacts, current_ref[t, 0:species], advected_ref[t])
        if first_x != 0:
            out_ref[t, 0:species] = result
            continue
        write = strided(out_ref)
        for values, shift in ((result, 0), (refs[10][t, 0:species], 2)):
            for k in range(2):
                x, y = divmod(2 * t + k, depth)
                write(y, x + shift)[...] = values[:, k * lanes : (k + 1) * lanes]


def half(first_x, shape, workers, *args):
    species, _, _, lanes = shape
    tiles = args[2].shape[0]
    block = (tiles, ROWS, 2 * lanes)
    smem = pl.BlockSpec(memory_space=pltpu.SMEM)
    return pl.pallas_call(
        functools.partial(half_kernel, first_x, workers),
        out_shape=jax.ShapeDtypeStruct(block if first_x else shape, jnp.float32),
        in_specs=[smem, smem] + [pl.BlockSpec() for _ in args[2:]],
        scratch_shapes=[
            pltpu.VMEM((tiles, species, 2 * lanes), jnp.float32),
            pltpu.VMEM(block, jnp.float32),
        ],
    )(*args)


def per_device(
    molar_fractions,
    fluid_speed_vector,
    thermal_state,
    molecular_spreading,
    arrhenius_ln_amplitude,
    arrhenius_energy,
    consumed_molecules,
    resulting_molecules,
    patch_assignee,
):
    species, width, depth, _ = molar_fractions.shape
    cells = molar_fractions.transpose(0, 2, 1, 3)
    flow_next, flow_back = ring("flow")
    chem_next, chem_back = ring("chem")
    xlo = lax.ppermute(cells[:, :, width - 2 :], "flow", flow_next)
    xhi = lax.ppermute(cells[:, :, :2], "flow", flow_back)
    ylo = lax.ppermute(cells[:, depth - 2 :], "chem", chem_next)
    yhi = lax.ppermute(cells[:, :2], "chem", chem_back)

    workers = lax.axis_size("chem")
    place = lax.axis_index("chem").astype(jnp.int32).reshape(1)
    gather, change, field, spread, lower, upper = prepare(
        cells,
        fluid_speed_vector.transpose(0, 2, 1, 3),
        thermal_state.transpose(1, 0, 2),
        molecular_spreading.reshape(1, species),
        arrhenius_ln_amplitude.reshape(1, -1),
        arrhenius_energy.reshape(1, -1),
        consumed_molecules.T,
        resulting_molecules.T,
    )
    shared = (field, spread, gather, change)
    owners = (place, patch_assignee)
    upper = half(2, cells.shape, workers, *owners, upper, xhi, ylo, yhi, *shared)
    out = half(0, cells.shape, workers, *owners, lower, xlo, ylo, yhi, *shared, upper)
    return out.transpose(0, 2, 1, 3)


def solution(mesh):
    in_specs = (
        P(None, "flow", "chem", None),
        P(None, "flow", "chem", None),
        P("flow", "chem", None),
        P(),
        P(),
        P(),
        P(),
        P(),
        P("flow", None),
    )
    out_specs = P(None, "flow", "chem", None)
    return jax.shard_map(
        per_device, mesh=mesh, in_specs=in_specs, out_specs=out_specs, check_vma=False
    )
```

```python
import functools

import jax
import jax.numpy as jnp
from jax import lax
from jax.experimental import pallas as pl
from jax.experimental.pallas import tpu as pltpu
from jax.sharding import PartitionSpec as P

PATCHES_ON_UNIT = 14
SUBSTEPS = 4
LOG2E = 1.4426950408889634
CONC_FLOOR = 0.1
CHEM_DT = 0.04
ROWS = 64
CHUNK = 128
UNROLL = 4


def ring(axis):
    count = lax.axis_size(axis)
    forward = [(i, (i + 1) % count) for i in range(count)]
    return forward, [(target, source) for source, target in forward]


def on_chip(values):
    return pltpu.with_memory_space_constraint(values, pltpu.VMEM)


def chunks(count):
    padded = -(-count // 16) * 16
    return [(start, min(CHUNK, padded - start)) for start in range(0, padded, CHUNK)]


def split(values):
    high = values.astype(jnp.bfloat16)
    low = (values - high.astype(jnp.float32)).astype(jnp.bfloat16)
    return jnp.concatenate([high, low], axis=0)


def pieces(values):
    high = values.astype(jnp.bfloat16).astype(jnp.float32)
    middle = (values - high).astype(jnp.bfloat16).astype(jnp.float32)
    return high, middle, values - high - middle


def strided(ref):
    species, ys, xs, lanes = ref.shape
    flat = ref.reshape(species * ys * xs, lanes)
    return lambda y, x: flat.at[pl.ds(y * xs + x, species, stride=ys * xs), :]


def prepare_kernel(
    u_ref, speed_ref, heat_ref, spread_ref, amplitude_ref, energy_ref, consumed_ref, resulting_ref,
    gather_ref, change_ref, field_ref, slow_ref, lower_ref, upper_ref, wide_ref, index_ref, rate_ref
):
    species, depth, width, lanes = u_ref.shape
    count = consumed_ref.shape[1]
    reach = index_ref.shape[1]
    slab = wide_ref.shape[1]
    stride = depth + 4

    index_ref[...] = jnp.full(index_ref.shape, -1, jnp.int32)
    index_ref[0:2, 0:count] = consumed_ref[...]
    index_ref[2:4, 0:count] = resulting_ref[...]
    rate_ref[...] = jnp.zeros_like(rate_ref)
    rate_ref[0:1, 0:count] = amplitude_ref[...] * LOG2E
    rate_ref[1:2, 0:count] = energy_ref[...] * -LOG2E
    ids = lax.broadcasted_iota(jnp.int32, (ROWS, reach), 0)
    ones = [jnp.where(index_ref[k : k + 1] == ids, 1.0, 0.0) for k in range(4)]
    used = ones[0] + ones[1]
    change = ones[2] + ones[3] - used
    a_high, a_middle, a_low = pieces(rate_ref[0:1])
    e_high, e_middle, e_low = pieces(rate_ref[1:2])
    for k, row in enumerate((a_high, e_high, a_middle, a_low, e_middle, e_low)):
        used = jnp.where(ids == species + k, row, used)
    both = jnp.concatenate([used, used], axis=0)
    rows = gather_ref.shape[0]
    for start in range(0, reach, lanes):
        size = min(lanes, rows - start)
        part = jnp.transpose(both[:, start : start + lanes])
        gather_ref[start : start + size] = part[0:size].astype(jnp.bfloat16)
    lane = lax.broadcasted_iota(jnp.int32, (ROWS, 2 * CHUNK), 1)
    for j, (start, size) in enumerate(chunks(count)):
        part = change[:, start : start + CHUNK]
        pair = jnp.concatenate([part, jnp.zeros_like(part)], axis=1)
        pair = jnp.where(lane < size, pair, 0.0)
        change_ref[j] = (pair + pltpu.roll(pair, size, 1)).astype(jnp.bfloat16)

    half = width // 2 * depth // 2
    for x in range(width):
        for y in range(depth):
            t, k = divmod(x * depth + y, 2)
            part = slice(k * lanes, (k + 1) * lanes)
            for c in range(3):
                field_ref[t, c : c + 1, part] = speed_ref[c, y, x : x + 1, :] * (1.0 / 12.0)
            field_ref[t, 3:4, part] = 1.0 / heat_ref[y, x : x + 1, :]
    spread = jnp.concatenate([spread_ref[...], jnp.zeros((1, lanes - species), jnp.float32)], axis=1)
    spread = jnp.transpose(jnp.broadcast_to(spread * (1.0 / 12.0), (lanes, lanes)))[0:slab]
    slow_ref[...] = spread

    for slot in range(width + 4):
        for y in range(stride):
            if 2 <= slot < width + 2 and 2 <= y < depth + 2:
                wide_ref[slot * stride + y, 0:species, :] = strided(u_ref)(y - 2, slot - 2)[...]
            elif 2 <= slot < width + 2 or 2 <= y < depth + 2:
                wide_ref[slot * stride + y] = jnp.zeros((slab, lanes), jnp.float32)

    def advect(row, field):
        x = row // depth
        y = row - x * depth
        base = (x + 2) * stride + y + 2
        center = wide_ref[base]
        near = jnp.zeros_like(center)
        far = jnp.zeros_like(center)
        moved = jnp.zeros_like(center)
        for axis in range(3):
            if axis == 2:
                low2 = pltpu.roll(center, 2, 1)
                low1 = pltpu.roll(center, 1, 1)
                high1 = pltpu.roll(center, lanes - 1, 1)
                high2 = pltpu.roll(center, lanes - 2, 1)
            else:
                hop = stride if axis == 0 else 1
                low2 = wide_ref[base - 2 * hop]
                low1 = wide_ref[base - hop]
                high1 = wide_ref[base + hop]
                high2 = wide_ref[base + 2 * hop]
            moved = moved + field[axis : axis + 1] * (8.0 * (high1 - low1) - (high2 - low2))
            near = near + (high1 + low1)
            far = far + (high2 + low2)
        return center - moved + spread * (16.0 * near - far - 90.0 * center)

    for target, shift in ((lower_ref, 0), (upper_ref, half)):
        def tile(t, carry, target=target, shift=shift):
            for k in range(2):
                part = slice(k * lanes, (k + 1) * lanes)
                target[t, 0:slab, part] = advect(2 * (t + shift) + k, field_ref[t + shift, :, part])
            target[t, slab:ROWS] = jnp.zeros((ROWS - slab, 2 * lanes), jnp.float32)
            return carry

        lax.fori_loop(0, half, tile, 0)


def prepare(cells, speed, heat, spread, amplitude, energy, consumed, resulting):
    species, depth, width, lanes = cells.shape
    count = consumed.shape[1]
    parts = chunks(count)
    reach = len(parts) * CHUNK
    slab = -(-species // 8) * 8
    tiles = width * depth // 2
    shapes = [
        ((parts[-1][0] + parts[-1][1], 2 * ROWS), jnp.bfloat16),
        ((len(parts), ROWS, 2 * CHUNK), jnp.bfloat16),
        ((tiles, 8, 2 * lanes), jnp.float32),
        ((slab, lanes), jnp.float32),
        ((tiles // 2, ROWS, 2 * lanes), jnp.float32),
        ((tiles // 2, ROWS, 2 * lanes), jnp.float32),
    ]
    return pl.pallas_call(
        prepare_kernel,
        out_shape=[pltpu.VMEM(*shape) for shape in shapes],
        scratch_shapes=[
            pltpu.VMEM(((width + 4) * (depth + 4), slab, lanes), jnp.float32),
            pltpu.VMEM((8, reach), jnp.int32),
            pltpu.VMEM((8, reach), jnp.float32),
        ],
        name="prepare",
    )(cells, speed, heat, spread, amplitude, energy, consumed, resulting)


def half_kernel(first_x, workers, *refs):
    place_ref, owner_ref, base_ref, side_ref, ylo_ref, yhi_ref, field_ref, spread_ref = refs[:8]
    gather_ref, change_ref = refs[8:10]
    out_ref, advected_ref, current_ref = refs[-3:]
    species, depth, _, lanes = side_ref.shape
    tiles = base_ref.shape[0]
    first_tile = first_x * depth // 2
    side, ylo, yhi = strided(side_ref), strided(ylo_ref), strided(yhi_ref)
    spread = spread_ref[0:species]

    for t in range(tiles):
        for k in range(2):
            x, y = divmod(2 * t + k, depth)
            part = slice(k * lanes, (k + 1) * lanes)
            field = field_ref[first_tile + t, :, part]
            values = base_ref[t, 0:species, part]

            def add(values, axis, far, value):
                speed = field[axis : axis + 1]
                if far > 0:
                    speed = -speed
                return values + (speed * 8.0 + spread * 16.0 if abs(far) == 1 else -speed - spread) * value

            if first_x == 0:
                taps = ((-2, 0), (-1, 1)) if x == 0 else ((-2, 1),)
            else:
                taps = ((2, 0),) if x == 0 else ((1, 0), (2, 1))
            for far, plane in taps:
                values = add(values, 0, far, side(y, plane)[...])
            column = first_x + x
            if y == 0:
                values = add(values, 1, -2, ylo(0, column)[...])
            if y <= 1:
                values = add(values, 1, -1 - y, ylo(1, column)[...])
            if y >= depth - 2:
                values = add(values, 1, depth - y, yhi(0, column)[...])
            if y == depth - 1:
                values = add(values, 1, 2, yhi(1, column)[...])
            advected_ref[t, 0:species, part] = values
            current_ref[t, 0:species, part] = values
        current_ref[t, species:ROWS] = jnp.ones((ROWS - species, 2 * lanes), jnp.float32)

    row_ids = lax.broadcasted_iota(jnp.int32, (16, 2 * lanes), 0) + (ROWS - 16)
    is_species = row_ids < species
    is_one = (row_ids == species) | (row_ids == species + 2) | (row_ids == species + 3)
    is_heat = (row_ids == species + 1) | (row_ids == species + 4) | (row_ids == species + 5)

    def exponent(t):
        logged = jnp.log(jnp.maximum(current_ref[t], CONC_FLOOR)) * LOG2E
        spare = jnp.where(is_one, 1.0, jnp.where(is_heat, field_ref[first_tile + t, 3:4], 0.0))
        stacked = jnp.concatenate(
            [logged[: ROWS - 16], jnp.where(is_species, logged[ROWS - 16 :], spare)], axis=0
        )
        return jnp.dot(gather_ref[...], split(stacked), preferred_element_type=jnp.float32)

    def gained(powers):
        total = None
        for j, (start, size) in enumerate(chunks(powers.shape[0])):
            progress = jnp.exp2(jnp.minimum(powers[start : start + size], LOG2E))
            part = jnp.dot(
                change_ref[j, :, 0 : 2 * size], split(progress), preferred_element_type=jnp.float32
            )
            total = part if total is None else total + part
        return CHEM_DT * total

    def substeps(turns):
        order = [(i, t) for i in range(turns) for t in range(tiles)]
        ready = exponent(0)
        for n, (_, t) in enumerate(order):
            powers = ready
            if n + 1 < len(order):
                ready = exponent(order[n + 1][1])
            current_ref[t] = current_ref[t] + gained(powers)

    if UNROLL == SUBSTEPS:
        substeps(SUBSTEPS)
    else:
        def turn(i, carry):
            substeps(UNROLL)
            return carry

        lax.fori_loop(0, SUBSTEPS // UNROLL, turn, 0)

    for t in range(tiles):
        reacts = owner_ref[0, place_ref[0] * PATCHES_ON_UNIT + first_tile + t] < workers
        result = jnp.where(reacts, current_ref[t, 0:species], advected_ref[t])
        if first_x != 0:
            out_ref[t, 0:species] = result
            continue
        write = strided(out_ref)
        for values, shift in ((result, 0), (refs[10][t, 0:species], 2)):
            for k in range(2):
                x, y = divmod(2 * t + k, depth)
                write(y, x + shift)[...] = values[:, k * lanes : (k + 1) * lanes]


def half(first_x, shape, workers, *args):
    species, _, _, lanes = shape
    tiles = args[2].shape[0]
    block = (tiles, ROWS, 2 * lanes)
    smem = pl.BlockSpec(memory_space=pltpu.SMEM)
    return pl.pallas_call(
        functools.partial(half_kernel, first_x, workers),
        out_shape=pltpu.VMEM(block, jnp.float32) if first_x else jax.ShapeDtypeStruct(shape, jnp.float32),
        in_specs=[smem, smem] + [pl.BlockSpec() for _ in args[2:]],
        scratch_shapes=[
            pltpu.VMEM((tiles, species, 2 * lanes), jnp.float32),
            pltpu.VMEM(block, jnp.float32),
        ],
    )(*args)


def per_device(
    molar_fractions,
    fluid_speed_vector,
    thermal_state,
    molecular_spreading,
    arrhenius_ln_amplitude,
    arrhenius_energy,
    consumed_molecules,
    resulting_molecules,
    patch_assignee,
):
    species, width, depth, _ = molar_fractions.shape
    cells = molar_fractions.transpose(0, 2, 1, 3)
    flow_next, flow_back = ring("flow")
    chem_next, chem_back = ring("chem")
    xlo = lax.ppermute(cells[:, :, width - 2 :], "flow", flow_next)
    again = lax.optimization_barrier(cells)
    xhi = lax.ppermute(again[:, :, :2], "flow", flow_back)
    ylo = lax.ppermute(cells[:, depth - 2 :], "chem", chem_next)
    yhi = lax.ppermute(cells[:, :2], "chem", chem_back)

    workers = lax.axis_size("chem")
    place = lax.axis_index("chem").astype(jnp.int32).reshape(1)
    gather, change, field, spread, lower, upper = prepare(
        cells,
        fluid_speed_vector.transpose(0, 2, 1, 3),
        thermal_state.transpose(1, 0, 2),
        molecular_spreading.reshape(1, species),
        arrhenius_ln_amplitude.reshape(1, -1),
        arrhenius_energy.reshape(1, -1),
        consumed_molecules.T,
        resulting_molecules.T,
    )
    shared = tuple(map(on_chip, (field, spread, gather, change)))
    owners = (place, patch_assignee)
    xlo, xhi, ylo, yhi, lower, upper = map(on_chip, (xlo, xhi, ylo, yhi, lower, upper))
    upper = half(2, cells.shape, workers, *owners, upper, xhi, ylo, yhi, *shared)
    out = half(0, cells.shape, workers, *owners, lower, xlo, ylo, yhi, *shared, on_chip(upper))
    return out.transpose(0, 2, 1, 3)


def solution(mesh):
    in_specs = (
        P(None, "flow", "chem", None),
        P(None, "flow", "chem", None),
        P("flow", "chem", None),
        P(),
        P(),
        P(),
        P(),
        P(),
        P("flow", None),
    )
    out_specs = P(None, "flow", "chem", None)
    return jax.shard_map(
        per_device, mesh=mesh, in_specs=in_specs, out_specs=out_specs, check_vma=False
    )
```

```python
import functools

import jax
import jax.numpy as jnp
from jax import lax
from jax.experimental import pallas as pl
from jax.experimental.pallas import tpu as pltpu
from jax.sharding import PartitionSpec as P

PATCHES_ON_UNIT = 14
SUBSTEPS = 4
LOG2E = 1.4426950408889634
CONC_FLOOR = 0.1
CHEM_DT = 0.04
ROWS = 64
CHUNK = 128
VMEM_LIMIT = 12 << 20


def ring(axis):
    count = lax.axis_size(axis)
    forward = [(i, (i + 1) % count) for i in range(count)]
    return forward, [(target, source) for source, target in forward]


def on_chip(values):
    return pltpu.with_memory_space_constraint(values, pltpu.VMEM)


def chunks(count):
    padded = -(-count // 16) * 16
    return [(start, min(CHUNK, padded - start)) for start in range(0, padded, CHUNK)]


def split(values):
    high = values.astype(jnp.bfloat16)
    low = (values - high.astype(jnp.float32)).astype(jnp.bfloat16)
    return jnp.concatenate([high, low], axis=0)


def pieces(values):
    high = values.astype(jnp.bfloat16).astype(jnp.float32)
    middle = (values - high).astype(jnp.bfloat16).astype(jnp.float32)
    return high, middle, values - high - middle


def strided(ref):
    species, ys, xs, lanes = ref.shape
    flat = ref.reshape(species * ys * xs, lanes)
    return lambda y, x: flat.at[pl.ds(y * xs + x, species, stride=ys * xs), :]


def prepare_kernel(
    u_ref, speed_ref, heat_ref, spread_ref, amplitude_ref, energy_ref, consumed_ref, resulting_ref,
    gather_ref, change_ref, field_ref, slow_ref, lower_ref, middle_ref, edge_ref, wide_ref, index_ref, rate_ref
):
    species, depth, width, lanes = u_ref.shape
    count = consumed_ref.shape[1]
    reach = index_ref.shape[1]
    slab = wide_ref.shape[1]
    stride = depth + 4

    index_ref[...] = jnp.full(index_ref.shape, -1, jnp.int32)
    index_ref[0:2, 0:count] = consumed_ref[...]
    index_ref[2:4, 0:count] = resulting_ref[...]
    rate_ref[...] = jnp.zeros_like(rate_ref)
    rate_ref[0:1, 0:count] = amplitude_ref[...] * LOG2E
    rate_ref[1:2, 0:count] = energy_ref[...] * -LOG2E
    ids = lax.broadcasted_iota(jnp.int32, (ROWS, reach), 0)
    ones = [jnp.where(index_ref[k : k + 1] == ids, 1.0, 0.0) for k in range(4)]
    used = ones[0] + ones[1]
    change = ones[2] + ones[3] - used
    a_high, a_middle, a_low = pieces(rate_ref[0:1])
    e_high, e_middle, e_low = pieces(rate_ref[1:2])
    for k, row in enumerate((a_high, e_high, a_middle, a_low, e_middle, e_low)):
        used = jnp.where(ids == species + k, row, used)
    both = jnp.concatenate([used, used], axis=0)
    rows = gather_ref.shape[0]
    for start in range(0, reach, lanes):
        size = min(lanes, rows - start)
        part = jnp.transpose(both[:, start : start + lanes])
        gather_ref[start : start + size] = part[0:size].astype(jnp.bfloat16)
    lane = lax.broadcasted_iota(jnp.int32, (ROWS, 2 * CHUNK), 1)
    for j, (start, size) in enumerate(chunks(count)):
        part = change[:, start : start + CHUNK]
        pair = jnp.concatenate([part, jnp.zeros_like(part)], axis=1)
        pair = jnp.where(lane < size, pair, 0.0)
        change_ref[j] = (pair + pltpu.roll(pair, size, 1)).astype(jnp.bfloat16)

    for x in range(width):
        for y in range(depth):
            t, k = x // 2 * depth + y, x % 2
            part = slice(k * lanes, (k + 1) * lanes)
            for c in range(3):
                field_ref[t, c : c + 1, part] = speed_ref[c, y, x : x + 1, :] * (1.0 / 12.0)
            field_ref[t, 3:4, part] = 1.0 / heat_ref[y, x : x + 1, :]
    spread = jnp.concatenate([spread_ref[...], jnp.zeros((1, lanes - species), jnp.float32)], axis=1)
    spread = jnp.transpose(jnp.broadcast_to(spread * (1.0 / 12.0), (lanes, lanes)))[0:slab]
    slow_ref[...] = spread

    for slot in range(width + 4):
        for y in range(stride):
            if 2 <= slot < width + 2 and 2 <= y < depth + 2:
                wide_ref[slot * stride + y, 0:species, :] = strided(u_ref)(y - 2, slot - 2)[...]
            elif 2 <= slot < width + 2 or 2 <= y < depth + 2:
                wide_ref[slot * stride + y] = jnp.zeros((slab, lanes), jnp.float32)

    def advect(x, y, field):
        base = (x + 2) * stride + y + 2
        center = wide_ref[base]
        near = jnp.zeros_like(center)
        far = jnp.zeros_like(center)
        moved = jnp.zeros_like(center)
        for axis in range(3):
            if axis == 2:
                low2 = pltpu.roll(center, 2, 1)
                low1 = pltpu.roll(center, 1, 1)
                high1 = pltpu.roll(center, lanes - 1, 1)
                high2 = pltpu.roll(center, lanes - 2, 1)
            else:
                hop = stride if axis == 0 else 1
                low2 = wide_ref[base - 2 * hop]
                low1 = wide_ref[base - hop]
                high1 = wide_ref[base + hop]
                high2 = wide_ref[base + 2 * hop]
            moved = moved + field[axis : axis + 1] * (8.0 * (high1 - low1) - (high2 - low2))
            near = near + (high1 + low1)
            far = far + (high2 + low2)
        return center - moved + spread * (16.0 * near - far - 90.0 * center)

    skipped = middle_ref.shape[0]
    first = edge_ref.shape[0] // 2
    for target, x0, row in (
        (lower_ref, 0, lambda t: t),
        (middle_ref, 2, lambda t: t + first),
        (edge_ref, 2, lambda t: t + jnp.where(t >= first, skipped, 0)),
    ):
        def tile(t, carry, target=target, x0=x0, row=row):
            y = row(t)
            for k in range(2):
                part = slice(k * lanes, (k + 1) * lanes)
                target[t, 0:slab, part] = advect(x0 + k, y, field_ref[x0 // 2 * depth + y, :, part])
            target[t, slab:ROWS] = jnp.zeros((ROWS - slab, 2 * lanes), jnp.float32)
            return carry

        lax.fori_loop(0, target.shape[0], tile, 0)


def prepare(cells, speed, heat, spread, amplitude, energy, consumed, resulting):
    species, depth, width, lanes = cells.shape
    count = consumed.shape[1]
    parts = chunks(count)
    reach = len(parts) * CHUNK
    slab = -(-species // 8) * 8
    tiles = width * depth // 2
    shapes = [
        ((parts[-1][0] + parts[-1][1], 2 * ROWS), jnp.bfloat16),
        ((len(parts), ROWS, 2 * CHUNK), jnp.bfloat16),
        ((tiles, 8, 2 * lanes), jnp.float32),
        ((slab, lanes), jnp.float32),
        ((depth, ROWS, 2 * lanes), jnp.float32),
        ((depth - 4, ROWS, 2 * lanes), jnp.float32),
        ((4, ROWS, 2 * lanes), jnp.float32),
    ]
    return pl.pallas_call(
        prepare_kernel,
        out_shape=[pltpu.VMEM(*shape) for shape in shapes],
        scratch_shapes=[
            pltpu.VMEM(((width + 4) * (depth + 4), slab, lanes), jnp.float32),
            pltpu.VMEM((8, reach), jnp.int32),
            pltpu.VMEM((8, reach), jnp.float32),
        ],
        compiler_params=pltpu.CompilerParams(vmem_limit_bytes=VMEM_LIMIT),
        name="prepare",
    )(cells, speed, heat, spread, amplitude, energy, consumed, resulting)


def part_kernel(first_x, rows, workers, *refs):
    place_ref, owner_ref, base_ref, side_ref, ylo_ref, yhi_ref, field_ref, spread_ref = refs[:8]
    gather_ref, change_ref = refs[8:10]
    if first_x == 0:
        middle_ref, edge_ref, out_ref, advected_ref, current_ref, whole_ref, sems = refs[10:]
    else:
        out_ref, advected_ref, current_ref = refs[10:]
    species, depth, _, lanes = side_ref.shape
    tiles = len(rows)
    first_tile = first_x // 2 * depth
    side, ylo, yhi = strided(side_ref), strided(ylo_ref), strided(yhi_ref)
    spread = spread_ref[0:species]

    for t, y in enumerate(rows):
        for x in range(2):
            part = slice(x * lanes, (x + 1) * lanes)
            field = field_ref[first_tile + y, :, part]
            values = base_ref[t, 0:species, part]

            def add(values, axis, far, value):
                speed = field[axis : axis + 1]
                if far > 0:
                    speed = -speed
                return values + (speed * 8.0 + spread * 16.0 if abs(far) == 1 else -speed - spread) * value

            if first_x == 0:
                taps = ((-2, 0), (-1, 1)) if x == 0 else ((-2, 1),)
            else:
                taps = ((2, 0),) if x == 0 else ((1, 0), (2, 1))
            for far, plane in taps:
                values = add(values, 0, far, side(y, plane)[...])
            column = first_x + x
            if y == 0:
                values = add(values, 1, -2, ylo(0, column)[...])
            if y <= 1:
                values = add(values, 1, -1 - y, ylo(1, column)[...])
            if y >= depth - 2:
                values = add(values, 1, depth - y, yhi(0, column)[...])
            if y == depth - 1:
                values = add(values, 1, 2, yhi(1, column)[...])
            advected_ref[t, 0:species, part] = values
            current_ref[t, 0:species, part] = values
        current_ref[t, species:ROWS] = jnp.ones((ROWS - species, 2 * lanes), jnp.float32)

    row_ids = lax.broadcasted_iota(jnp.int32, (16, 2 * lanes), 0) + (ROWS - 16)
    is_species = row_ids < species
    is_one = (row_ids == species) | (row_ids == species + 2) | (row_ids == species + 3)
    is_heat = (row_ids == species + 1) | (row_ids == species + 4) | (row_ids == species + 5)

    def exponent(t):
        logged = jnp.log(jnp.maximum(current_ref[t], CONC_FLOOR)) * LOG2E
        spare = jnp.where(is_one, 1.0, jnp.where(is_heat, field_ref[first_tile + rows[t], 3:4], 0.0))
        stacked = jnp.concatenate(
            [logged[: ROWS - 16], jnp.where(is_species, logged[ROWS - 16 :], spare)], axis=0
        )
        return jnp.dot(gather_ref[...], split(stacked), preferred_element_type=jnp.float32)

    def gained(powers):
        total = None
        for j, (start, size) in enumerate(chunks(powers.shape[0])):
            progress = jnp.exp2(jnp.minimum(powers[start : start + size], LOG2E))
            part = jnp.dot(
                change_ref[j, :, 0 : 2 * size], split(progress), preferred_element_type=jnp.float32
            )
            total = part if total is None else total + part
        return CHEM_DT * total

    def settled(t):
        y = rows[t]
        picked = []
        for x in range(2):
            part = slice(x * lanes, (x + 1) * lanes)
            block = ((first_x + x) * depth + y) // 2
            reacts = owner_ref[0, place_ref[0] * PATCHES_ON_UNIT + block] < workers
            picked.append(jnp.where(reacts, current_ref[t, 0:species, part], advected_ref[t, :, part]))
        return picked

    copies = []
    if first_x == 0:
        write = strided(whole_ref)
        others = [middle_ref.at[y - 2] if 2 <= y < depth - 2 else edge_ref.at[y if y < 2 else y - depth + 4] for y in rows]
        for y in rows:
            for x in range(2):
                write(y, x + 2)[...] = others[y][0:species, x * lanes : (x + 1) * lanes]

    order = [(i, t) for i in range(SUBSTEPS) for t in range(tiles)]
    ready = exponent(0)
    for n, (i, t) in enumerate(order):
        powers = ready
        if n + 1 < len(order):
            ready = exponent(order[n + 1][1])
        current_ref[t] = current_ref[t] + gained(powers)
        if i + 1 < SUBSTEPS:
            continue
        picked = settled(t)
        for x in range(2):
            if first_x == 0:
                write(rows[t], x)[...] = picked[x]
            else:
                out_ref[t, 0:species, x * lanes : (x + 1) * lanes] = picked[x]
        if first_x == 0:
            y = rows[t]
            copies.append(pltpu.make_async_copy(whole_ref.at[:, y], out_ref.at[:, y], sems.at[t]))
            copies[-1].start()
    for copy in copies:
        copy.wait()


def part(first_x, rows, shape, workers, *args):
    species, _, _, lanes = shape
    tiles = len(rows)
    block = (tiles, ROWS, 2 * lanes)
    smem = pl.BlockSpec(memory_space=pltpu.SMEM)
    scratch = [
        pltpu.VMEM((tiles, species, 2 * lanes), jnp.float32),
        pltpu.VMEM(block, jnp.float32),
    ]
    if first_x == 0:
        scratch += [pltpu.VMEM(shape, jnp.float32), pltpu.SemaphoreType.DMA((tiles,))]
    return pl.pallas_call(
        functools.partial(part_kernel, first_x, rows, workers),
        out_shape=pltpu.VMEM(block, jnp.float32) if first_x else jax.ShapeDtypeStruct(shape, jnp.float32),
        in_specs=[smem, smem] + [pl.BlockSpec() for _ in args[2:]],
        out_specs=pl.BlockSpec() if first_x else pl.BlockSpec(memory_space=pl.ANY),
        scratch_shapes=scratch,
        compiler_params=pltpu.CompilerParams(vmem_limit_bytes=VMEM_LIMIT),
    )(*args)


def per_device(
    molar_fractions,
    fluid_speed_vector,
    thermal_state,
    molecular_spreading,
    arrhenius_ln_amplitude,
    arrhenius_energy,
    consumed_molecules,
    resulting_molecules,
    patch_assignee,
):
    species, width, depth, _ = molar_fractions.shape
    cells = molar_fractions.transpose(0, 2, 1, 3)
    flow_next, flow_back = ring("flow")
    chem_next, chem_back = ring("chem")
    xlo = lax.ppermute(cells[:, :, width - 2 :], "flow", flow_next)
    again = lax.optimization_barrier(cells)
    xhi = lax.ppermute(again[:, :, :2], "flow", flow_back)
    ylo = lax.ppermute(cells[:, depth - 2 :], "chem", chem_next)
    yhi = lax.ppermute(cells[:, :2], "chem", chem_back)

    workers = lax.axis_size("chem")
    place = lax.axis_index("chem").astype(jnp.int32).reshape(1)
    gather, change, field, spread, lower, middle, edge = prepare(
        cells,
        fluid_speed_vector.transpose(0, 2, 1, 3),
        thermal_state.transpose(1, 0, 2),
        molecular_spreading.reshape(1, species),
        arrhenius_ln_amplitude.reshape(1, -1),
        arrhenius_energy.reshape(1, -1),
        consumed_molecules.T,
        resulting_molecules.T,
    )
    shared = tuple(map(on_chip, (field, spread, gather, change)))
    owners = (place, patch_assignee)
    xlo, xhi, ylo, yhi, lower, middle, edge = map(on_chip, (xlo, xhi, ylo, yhi, lower, middle, edge))
    inner = tuple(range(2, depth - 2))
    outer = (0, 1, depth - 2, depth - 1)
    middle = part(2, inner, cells.shape, workers, *owners, middle, xhi, xhi, xhi, *shared)
    edge = part(2, outer, cells.shape, workers, *owners, edge, xhi, ylo, yhi, *shared)
    out = part(
        0, tuple(range(depth)), cells.shape, workers, *owners, lower, xlo, ylo, yhi, *shared,
        on_chip(middle), on_chip(edge)
    )
    return out.transpose(0, 2, 1, 3)


def solution(mesh):
    in_specs = (
        P(None, "flow", "chem", None),
        P(None, "flow", "chem", None),
        P("flow", "chem", None),
        P(),
        P(),
        P(),
        P(),
        P(),
        P("flow", None),
    )
    out_specs = P(None, "flow", "chem", None)
    return jax.shard_map(
        per_device, mesh=mesh, in_specs=in_specs, out_specs=out_specs, check_vma=False
    )
```

```python
import functools

import jax
import jax.numpy as jnp
from jax import lax
from jax.experimental import pallas as pl
from jax.experimental.pallas import tpu as pltpu
from jax.sharding import PartitionSpec as P

PATCHES_ON_UNIT = 14
SUBSTEPS = 4
LOG2E = 1.4426950408889634
CONC_FLOOR = 0.1
CHEM_DT = 0.04
ROWS = 64
CHUNK = 128
VMEM_LIMIT = 12 << 20


def ring(axis):
    count = lax.axis_size(axis)
    forward = [(i, (i + 1) % count) for i in range(count)]
    return forward, [(target, source) for source, target in forward]


def on_chip(values):
    return pltpu.with_memory_space_constraint(values, pltpu.VMEM)


def chunks(count):
    padded = -(-count // 16) * 16
    return [(start, min(CHUNK, padded - start)) for start in range(0, padded, CHUNK)]


def split(values):
    high = values.astype(jnp.bfloat16)
    low = (values - high.astype(jnp.float32)).astype(jnp.bfloat16)
    return jnp.concatenate([high, low], axis=0)


def pieces(values):
    high = values.astype(jnp.bfloat16).astype(jnp.float32)
    middle = (values - high).astype(jnp.bfloat16).astype(jnp.float32)
    return high, middle, values - high - middle


def strided(ref):
    species, ys, xs, lanes = ref.shape
    flat = ref.reshape(species * ys * xs, lanes)
    return lambda y, x: flat.at[pl.ds(y * xs + x, species, stride=ys * xs), :]


def prepare_kernel(
    workers, place_ref, owner_ref, u_ref, speed_ref, heat_ref, spread_ref, amplitude_ref, energy_ref, consumed_ref, resulting_ref,
    gather_ref, change_ref, field_ref, slow_ref, lower_ref, middle_ref, edge_ref, wide_ref, index_ref, rate_ref
):
    species, depth, width, lanes = u_ref.shape
    count = consumed_ref.shape[1]
    reach = index_ref.shape[1]
    slab = wide_ref.shape[1]
    stride = depth + 4

    index_ref[...] = jnp.full(index_ref.shape, -1, jnp.int32)
    index_ref[0:2, 0:count] = consumed_ref[...]
    index_ref[2:4, 0:count] = resulting_ref[...]
    rate_ref[...] = jnp.zeros_like(rate_ref)
    rate_ref[0:1, 0:count] = amplitude_ref[...] * LOG2E
    rate_ref[1:2, 0:count] = energy_ref[...] * -LOG2E
    ids = lax.broadcasted_iota(jnp.int32, (ROWS, reach), 0)
    ones = [jnp.where(index_ref[k : k + 1] == ids, 1.0, 0.0) for k in range(4)]
    used = ones[0] + ones[1]
    change = ones[2] + ones[3] - used
    a_high, a_middle, a_low = pieces(rate_ref[0:1])
    e_high, e_middle, e_low = pieces(rate_ref[1:2])
    for k, row in enumerate((a_high, e_high, a_middle, a_low, e_middle, e_low)):
        used = jnp.where(ids == species + k, row, used)
    both = jnp.concatenate([used, used], axis=0)
    rows = gather_ref.shape[0]
    for start in range(0, reach, lanes):
        size = min(lanes, rows - start)
        part = jnp.transpose(both[:, start : start + lanes])
        gather_ref[start : start + size] = part[0:size].astype(jnp.bfloat16)
    lane = lax.broadcasted_iota(jnp.int32, (ROWS, 2 * CHUNK), 1)
    for j, (start, size) in enumerate(chunks(count)):
        part = change[:, start : start + CHUNK]
        pair = jnp.concatenate([part, jnp.zeros_like(part)], axis=1)
        pair = jnp.where(lane < size, pair, 0.0)
        change_ref[j] = (pair + pltpu.roll(pair, size, 1)).astype(jnp.bfloat16)

    for x in range(width):
        for y in range(depth):
            t, k = x // 2 * depth + y, x % 2
            part = slice(k * lanes, (k + 1) * lanes)
            for c in range(3):
                field_ref[t, c : c + 1, part] = speed_ref[c, y, x : x + 1, :] * (1.0 / 12.0)
            field_ref[t, 3:4, part] = 1.0 / heat_ref[y, x : x + 1, :]
            block = place_ref[0] * PATCHES_ON_UNIT + (x * depth + y) // 2
            reacts = jnp.where(owner_ref[0, block] < workers, 1.0, 0.0)
            field_ref[t, 4:5, part] = jnp.full((1, lanes), reacts, jnp.float32)
    spread = jnp.concatenate([spread_ref[...], jnp.zeros((1, lanes - species), jnp.float32)], axis=1)
    spread = jnp.transpose(jnp.broadcast_to(spread * (1.0 / 12.0), (lanes, lanes)))[0:slab]
    slow_ref[...] = spread

    for slot in range(width + 4):
        for y in range(stride):
            if 2 <= slot < width + 2 and 2 <= y < depth + 2:
                wide_ref[slot * stride + y, 0:species, :] = strided(u_ref)(y - 2, slot - 2)[...]
            elif 2 <= slot < width + 2 or 2 <= y < depth + 2:
                wide_ref[slot * stride + y] = jnp.zeros((slab, lanes), jnp.float32)

    def advect(x, y, field):
        base = (x + 2) * stride + y + 2
        center = wide_ref[base]
        near = jnp.zeros_like(center)
        far = jnp.zeros_like(center)
        moved = jnp.zeros_like(center)
        for axis in range(3):
            if axis == 2:
                low2 = pltpu.roll(center, 2, 1)
                low1 = pltpu.roll(center, 1, 1)
                high1 = pltpu.roll(center, lanes - 1, 1)
                high2 = pltpu.roll(center, lanes - 2, 1)
            else:
                hop = stride if axis == 0 else 1
                low2 = wide_ref[base - 2 * hop]
                low1 = wide_ref[base - hop]
                high1 = wide_ref[base + hop]
                high2 = wide_ref[base + 2 * hop]
            moved = moved + field[axis : axis + 1] * (8.0 * (high1 - low1) - (high2 - low2))
            near = near + (high1 + low1)
            far = far + (high2 + low2)
        return center - moved + spread * (16.0 * near - far - 90.0 * center)

    skipped = middle_ref.shape[0]
    first = edge_ref.shape[0] // 2
    for target, x0, row in (
        (lower_ref, 0, lambda t: t),
        (middle_ref, 2, lambda t: t + first),
        (edge_ref, 2, lambda t: t + jnp.where(t >= first, skipped, 0)),
    ):
        def tile(t, carry, target=target, x0=x0, row=row):
            y = row(t)
            for k in range(2):
                part = slice(k * lanes, (k + 1) * lanes)
                target[t, 0:slab, part] = advect(x0 + k, y, field_ref[x0 // 2 * depth + y, :, part])
            target[t, slab:ROWS] = jnp.zeros((ROWS - slab, 2 * lanes), jnp.float32)
            return carry

        lax.fori_loop(0, target.shape[0], tile, 0)


def prepare(workers, place, owners, cells, *args):
    consumed = args[-1]
    species, depth, width, lanes = cells.shape
    count = consumed.shape[1]
    parts = chunks(count)
    reach = len(parts) * CHUNK
    slab = -(-species // 8) * 8
    tiles = width * depth // 2
    shapes = [
        ((parts[-1][0] + parts[-1][1], 2 * ROWS), jnp.bfloat16),
        ((len(parts), ROWS, 2 * CHUNK), jnp.bfloat16),
        ((tiles, 8, 2 * lanes), jnp.float32),
        ((slab, lanes), jnp.float32),
        ((depth, ROWS, 2 * lanes), jnp.float32),
        ((depth - 4, ROWS, 2 * lanes), jnp.float32),
        ((4, ROWS, 2 * lanes), jnp.float32),
    ]
    return pl.pallas_call(
        functools.partial(prepare_kernel, workers),
        out_shape=[pltpu.VMEM(*shape) for shape in shapes],
        in_specs=[pl.BlockSpec(memory_space=pltpu.SMEM)] * 2 + [pl.BlockSpec()] * (1 + len(args)),
        scratch_shapes=[
            pltpu.VMEM(((width + 4) * (depth + 4), slab, lanes), jnp.float32),
            pltpu.VMEM((8, reach), jnp.int32),
            pltpu.VMEM((8, reach), jnp.float32),
        ],
        compiler_params=pltpu.CompilerParams(vmem_limit_bytes=VMEM_LIMIT),
        name="prepare",
    )(place, owners, cells, *args)


def part_kernel(first_x, rows, *refs):
    base_ref, side_ref, ylo_ref, yhi_ref, field_ref, spread_ref, gather_ref, change_ref = refs[:8]
    if first_x == 0:
        middle_ref, edge_ref, out_ref, advected_ref, current_ref, whole_ref, sems = refs[8:]
    else:
        out_ref, advected_ref, current_ref = refs[8:]
    species, depth, _, lanes = side_ref.shape
    tiles = len(rows)
    first_tile = first_x // 2 * depth
    side, ylo, yhi = strided(side_ref), strided(ylo_ref), strided(yhi_ref)
    spread = spread_ref[0:species]

    for t, y in enumerate(rows):
        for x in range(2):
            part = slice(x * lanes, (x + 1) * lanes)
            field = field_ref[first_tile + y, :, part]
            values = base_ref[t, 0:species, part]

            def add(values, axis, far, value):
                speed = field[axis : axis + 1]
                if far > 0:
                    speed = -speed
                return values + (speed * 8.0 + spread * 16.0 if abs(far) == 1 else -speed - spread) * value

            if first_x == 0:
                taps = ((-2, 0), (-1, 1)) if x == 0 else ((-2, 1),)
            else:
                taps = ((2, 0),) if x == 0 else ((1, 0), (2, 1))
            for far, plane in taps:
                values = add(values, 0, far, side(y, plane)[...])
            column = first_x + x
            if y == 0:
                values = add(values, 1, -2, ylo(0, column)[...])
            if y <= 1:
                values = add(values, 1, -1 - y, ylo(1, column)[...])
            if y >= depth - 2:
                values = add(values, 1, depth - y, yhi(0, column)[...])
            if y == depth - 1:
                values = add(values, 1, 2, yhi(1, column)[...])
            advected_ref[t, 0:species, part] = values
            current_ref[t, 0:species, part] = values
        current_ref[t, species:ROWS] = jnp.ones((ROWS - species, 2 * lanes), jnp.float32)

    row_ids = lax.broadcasted_iota(jnp.int32, (16, 2 * lanes), 0) + (ROWS - 16)
    is_species = row_ids < species
    is_one = (row_ids == species) | (row_ids == species + 2) | (row_ids == species + 3)
    is_heat = (row_ids == species + 1) | (row_ids == species + 4) | (row_ids == species + 5)

    def exponent(t):
        logged = jnp.log(jnp.maximum(current_ref[t], CONC_FLOOR)) * LOG2E
        spare = jnp.where(is_one, 1.0, jnp.where(is_heat, field_ref[first_tile + rows[t], 3:4], 0.0))
        stacked = jnp.concatenate(
            [logged[: ROWS - 16], jnp.where(is_species, logged[ROWS - 16 :], spare)], axis=0
        )
        return jnp.dot(gather_ref[...], split(stacked), preferred_element_type=jnp.float32)

    def gained(powers):
        total = None
        for j, (start, size) in enumerate(chunks(powers.shape[0])):
            progress = jnp.exp2(jnp.minimum(powers[start : start + size], LOG2E))
            part = jnp.dot(
                change_ref[j, :, 0 : 2 * size], split(progress), preferred_element_type=jnp.float32
            )
            total = part if total is None else total + part
        return CHEM_DT * total

    def settled(t):
        y = rows[t]
        picked = []
        for x in range(2):
            part = slice(x * lanes, (x + 1) * lanes)
            reacts = field_ref[first_tile + y, 4:5, part] > 0.5
            picked.append(jnp.where(reacts, current_ref[t, 0:species, part], advected_ref[t, :, part]))
        return picked

    copies = []
    if first_x == 0:
        write = strided(whole_ref)
        others = [middle_ref.at[y - 2] if 2 <= y < depth - 2 else edge_ref.at[y if y < 2 else y - depth + 4] for y in rows]
        for y in rows:
            for x in range(2):
                write(y, x + 2)[...] = others[y][0:species, x * lanes : (x + 1) * lanes]

    order = [(i, t) for i in range(SUBSTEPS) for t in range(tiles)]
    ready = exponent(0)
    for n, (i, t) in enumerate(order):
        powers = ready
        if n + 1 < len(order):
            ready = exponent(order[n + 1][1])
        current_ref[t] = current_ref[t] + gained(powers)
        if i + 1 < SUBSTEPS:
            continue
        picked = settled(t)
        for x in range(2):
            if first_x == 0:
                write(rows[t], x)[...] = picked[x]
            else:
                out_ref[t, 0:species, x * lanes : (x + 1) * lanes] = picked[x]
        if first_x == 0:
            y = rows[t]
            copies.append(pltpu.make_async_copy(whole_ref.at[:, y], out_ref.at[:, y], sems.at[t]))
            copies[-1].start()
    for copy in copies:
        copy.wait()


def part(first_x, rows, shape, *args):
    species, _, _, lanes = shape
    tiles = len(rows)
    block = (tiles, ROWS, 2 * lanes)
    scratch = [
        pltpu.VMEM((tiles, species, 2 * lanes), jnp.float32),
        pltpu.VMEM(block, jnp.float32),
    ]
    if first_x == 0:
        scratch += [pltpu.VMEM(shape, jnp.float32), pltpu.SemaphoreType.DMA((tiles,))]
    return pl.pallas_call(
        functools.partial(part_kernel, first_x, rows),
        out_shape=pltpu.VMEM(block, jnp.float32) if first_x else jax.ShapeDtypeStruct(shape, jnp.float32),
        out_specs=pl.BlockSpec() if first_x else pl.BlockSpec(memory_space=pl.ANY),
        scratch_shapes=scratch,
        compiler_params=pltpu.CompilerParams(vmem_limit_bytes=VMEM_LIMIT),
    )(*args)


def per_device(
    molar_fractions,
    fluid_speed_vector,
    thermal_state,
    molecular_spreading,
    arrhenius_ln_amplitude,
    arrhenius_energy,
    consumed_molecules,
    resulting_molecules,
    patch_assignee,
):
    species, width, depth, _ = molar_fractions.shape
    cells = molar_fractions.transpose(0, 2, 1, 3)
    flow_next, flow_back = ring("flow")
    chem_next, chem_back = ring("chem")
    xlo = lax.ppermute(cells[:, :, width - 2 :], "flow", flow_next)
    again = lax.optimization_barrier(cells)
    xhi = lax.ppermute(again[:, :, :2], "flow", flow_back)
    ylo = lax.ppermute(cells[:, depth - 2 :], "chem", chem_next)
    yhi = lax.ppermute(cells[:, :2], "chem", chem_back)

    workers = lax.axis_size("chem")
    place = lax.axis_index("chem").astype(jnp.int32).reshape(1)
    gather, change, field, spread, lower, middle, edge = prepare(
        workers,
        place,
        patch_assignee,
        cells,
        fluid_speed_vector.transpose(0, 2, 1, 3),
        thermal_state.transpose(1, 0, 2),
        molecular_spreading.reshape(1, species),
        arrhenius_ln_amplitude.reshape(1, -1),
        arrhenius_energy.reshape(1, -1),
        consumed_molecules.T,
        resulting_molecules.T,
    )
    shared = tuple(map(on_chip, (field, spread, gather, change)))
    xlo, xhi, ylo, yhi, lower, middle, edge = map(on_chip, (xlo, xhi, ylo, yhi, lower, middle, edge))
    inner = tuple(range(2, depth - 2))
    outer = (0, 1, depth - 2, depth - 1)
    middle = part(2, inner, cells.shape, middle, xhi, xhi, xhi, *shared)
    edge = part(2, outer, cells.shape, edge, xhi, ylo, yhi, *shared)
    out = part(
        0, tuple(range(depth)), cells.shape, lower, xlo, ylo, yhi, *shared,
        on_chip(middle), on_chip(edge)
    )
    return out.transpose(0, 2, 1, 3)


def solution(mesh):
    in_specs = (
        P(None, "flow", "chem", None),
        P(None, "flow", "chem", None),
        P("flow", "chem", None),
        P(),
        P(),
        P(),
        P(),
        P(),
        P("flow", None),
    )
    out_specs = P(None, "flow", "chem", None)
    return jax.shard_map(
        per_device, mesh=mesh, in_specs=in_specs, out_specs=out_specs, check_vma=False
    )
```

```python
import functools

import jax
import jax.numpy as jnp
from jax import lax
from jax.experimental import pallas as pl
from jax.experimental.pallas import tpu as pltpu
from jax.sharding import PartitionSpec as P

PATCHES_ON_UNIT = 14
SUBSTEPS = 4
LOG2E = 1.4426950408889634
CONC_FLOOR = 0.1
CHEM_DT = 0.04
ROWS = 64
CHUNK = 128
VMEM_LIMIT = 12 << 20


def ring(axis):
    count = lax.axis_size(axis)
    forward = [(i, (i + 1) % count) for i in range(count)]
    return forward, [(target, source) for source, target in forward]


def on_chip(values):
    return pltpu.with_memory_space_constraint(values, pltpu.VMEM)


def chunks(count):
    padded = -(-count // 16) * 16
    return [(start, min(CHUNK, padded - start)) for start in range(0, padded, CHUNK)]


def split(values):
    high = values.astype(jnp.bfloat16)
    low = (values - high.astype(jnp.float32)).astype(jnp.bfloat16)
    return jnp.concatenate([high, low], axis=0)


def pieces(values):
    high = values.astype(jnp.bfloat16).astype(jnp.float32)
    middle = (values - high).astype(jnp.bfloat16).astype(jnp.float32)
    return high, middle, values - high - middle


def strided(ref):
    species, ys, xs, lanes = ref.shape
    flat = ref.reshape(species * ys * xs, lanes)
    return lambda y, x: flat.at[pl.ds(y * xs + x, species, stride=ys * xs), :]


def cut_kernel(cells_ref, out_ref, sem):
    copy = pltpu.make_async_copy(cells_ref.at[:, :, cells_ref.shape[2] - 2 :], out_ref, sem)
    copy.start()
    copy.wait()


def last_planes(cells):
    species, depth, _, lanes = cells.shape
    return pl.pallas_call(
        cut_kernel,
        out_shape=pltpu.VMEM((species, depth, 2, lanes), jnp.float32),
        in_specs=[pl.BlockSpec(memory_space=pl.ANY)],
        scratch_shapes=[pltpu.SemaphoreType.DMA],
        compiler_params=pltpu.CompilerParams(vmem_limit_bytes=VMEM_LIMIT),
        name="cut",
    )(cells)


def prepare_kernel(
    workers, place_ref, owner_ref, u_ref, speed_ref, heat_ref, spread_ref, amplitude_ref, energy_ref, consumed_ref, resulting_ref,
    gather_ref, change_ref, field_ref, slow_ref, lower_ref, middle_ref, edge_ref, wide_ref, index_ref, rate_ref
):
    species, depth, width, lanes = u_ref.shape
    count = consumed_ref.shape[1]
    reach = index_ref.shape[1]
    slab = wide_ref.shape[1]
    stride = depth + 4

    index_ref[...] = jnp.full(index_ref.shape, -1, jnp.int32)
    index_ref[0:2, 0:count] = consumed_ref[...]
    index_ref[2:4, 0:count] = resulting_ref[...]
    rate_ref[...] = jnp.zeros_like(rate_ref)
    rate_ref[0:1, 0:count] = amplitude_ref[...] * LOG2E
    rate_ref[1:2, 0:count] = energy_ref[...] * -LOG2E
    ids = lax.broadcasted_iota(jnp.int32, (ROWS, reach), 0)
    ones = [jnp.where(index_ref[k : k + 1] == ids, 1.0, 0.0) for k in range(4)]
    used = ones[0] + ones[1]
    change = ones[2] + ones[3] - used
    a_high, a_middle, a_low = pieces(rate_ref[0:1])
    e_high, e_middle, e_low = pieces(rate_ref[1:2])
    for k, row in enumerate((a_high, e_high, a_middle, a_low, e_middle, e_low)):
        used = jnp.where(ids == species + k, row, used)
    both = jnp.concatenate([used, used], axis=0)
    rows = gather_ref.shape[0]
    for start in range(0, reach, lanes):
        size = min(lanes, rows - start)
        part = jnp.transpose(both[:, start : start + lanes])
        gather_ref[start : start + size] = part[0:size].astype(jnp.bfloat16)
    lane = lax.broadcasted_iota(jnp.int32, (ROWS, 2 * CHUNK), 1)
    for j, (start, size) in enumerate(chunks(count)):
        part = change[:, start : start + CHUNK]
        pair = jnp.concatenate([part, jnp.zeros_like(part)], axis=1)
        pair = jnp.where(lane < size, pair, 0.0)
        change_ref[j] = (pair + pltpu.roll(pair, size, 1)).astype(jnp.bfloat16)

    for x in range(width):
        for y in range(depth):
            t, k = x // 2 * depth + y, x % 2
            part = slice(k * lanes, (k + 1) * lanes)
            for c in range(3):
                field_ref[t, c : c + 1, part] = speed_ref[c, y, x : x + 1, :] * (1.0 / 12.0)
            field_ref[t, 3:4, part] = 1.0 / heat_ref[y, x : x + 1, :]
            block = place_ref[0] * PATCHES_ON_UNIT + (x * depth + y) // 2
            reacts = jnp.where(owner_ref[0, block] < workers, 1.0, 0.0)
            field_ref[t, 4:5, part] = jnp.full((1, lanes), reacts, jnp.float32)
    spread = jnp.concatenate([spread_ref[...], jnp.zeros((1, lanes - species), jnp.float32)], axis=1)
    spread = jnp.transpose(jnp.broadcast_to(spread * (1.0 / 12.0), (lanes, lanes)))[0:slab]
    slow_ref[...] = spread

    for slot in range(width + 4):
        for y in range(stride):
            if 2 <= slot < width + 2 and 2 <= y < depth + 2:
                wide_ref[slot * stride + y, 0:species, :] = strided(u_ref)(y - 2, slot - 2)[...]
            elif 2 <= slot < width + 2 or 2 <= y < depth + 2:
                wide_ref[slot * stride + y] = jnp.zeros((slab, lanes), jnp.float32)

    def advect(x, y, field):
        base = (x + 2) * stride + y + 2
        center = wide_ref[base]
        near = jnp.zeros_like(center)
        far = jnp.zeros_like(center)
        moved = jnp.zeros_like(center)
        for axis in range(3):
            if axis == 2:
                low2 = pltpu.roll(center, 2, 1)
                low1 = pltpu.roll(center, 1, 1)
                high1 = pltpu.roll(center, lanes - 1, 1)
                high2 = pltpu.roll(center, lanes - 2, 1)
            else:
                hop = stride if axis == 0 else 1
                low2 = wide_ref[base - 2 * hop]
                low1 = wide_ref[base - hop]
                high1 = wide_ref[base + hop]
                high2 = wide_ref[base + 2 * hop]
            moved = moved + field[axis : axis + 1] * (8.0 * (high1 - low1) - (high2 - low2))
            near = near + (high1 + low1)
            far = far + (high2 + low2)
        return center - moved + spread * (16.0 * near - far - 90.0 * center)

    skipped = middle_ref.shape[0]
    first = edge_ref.shape[0] // 2
    for target, x0, row in (
        (lower_ref, 0, lambda t: t),
        (middle_ref, 2, lambda t: t + first),
        (edge_ref, 2, lambda t: t + jnp.where(t >= first, skipped, 0)),
    ):
        def tile(t, carry, target=target, x0=x0, row=row):
            y = row(t)
            for k in range(2):
                part = slice(k * lanes, (k + 1) * lanes)
                target[t, 0:slab, part] = advect(x0 + k, y, field_ref[x0 // 2 * depth + y, :, part])
            target[t, slab:ROWS] = jnp.zeros((ROWS - slab, 2 * lanes), jnp.float32)
            return carry

        lax.fori_loop(0, target.shape[0], tile, 0)


def prepare(workers, place, owners, cells, *args):
    consumed = args[-1]
    species, depth, width, lanes = cells.shape
    count = consumed.shape[1]
    parts = chunks(count)
    reach = len(parts) * CHUNK
    slab = -(-species // 8) * 8
    tiles = width * depth // 2
    shapes = [
        ((parts[-1][0] + parts[-1][1], 2 * ROWS), jnp.bfloat16),
        ((len(parts), ROWS, 2 * CHUNK), jnp.bfloat16),
        ((tiles, 8, 2 * lanes), jnp.float32),
        ((slab, lanes), jnp.float32),
        ((depth, ROWS, 2 * lanes), jnp.float32),
        ((depth - 4, ROWS, 2 * lanes), jnp.float32),
        ((4, ROWS, 2 * lanes), jnp.float32),
    ]
    return pl.pallas_call(
        functools.partial(prepare_kernel, workers),
        out_shape=[pltpu.VMEM(*shape) for shape in shapes],
        in_specs=[pl.BlockSpec(memory_space=pltpu.SMEM)] * 2 + [pl.BlockSpec()] * (1 + len(args)),
        scratch_shapes=[
            pltpu.VMEM(((width + 4) * (depth + 4), slab, lanes), jnp.float32),
            pltpu.VMEM((8, reach), jnp.int32),
            pltpu.VMEM((8, reach), jnp.float32),
        ],
        compiler_params=pltpu.CompilerParams(vmem_limit_bytes=VMEM_LIMIT),
        name="prepare",
    )(place, owners, cells, *args)


def part_kernel(first_x, rows, *refs):
    base_ref, side_ref, ylo_ref, yhi_ref, field_ref, spread_ref, gather_ref, change_ref = refs[:8]
    if first_x == 0:
        middle_ref, edge_ref, out_ref, advected_ref, current_ref, whole_ref, sems = refs[8:]
    else:
        out_ref, advected_ref, current_ref = refs[8:]
    species, depth, _, lanes = side_ref.shape
    tiles = len(rows)
    first_tile = first_x // 2 * depth
    side, ylo, yhi = strided(side_ref), strided(ylo_ref), strided(yhi_ref)
    spread = spread_ref[0:species]

    for t, y in enumerate(rows):
        for x in range(2):
            part = slice(x * lanes, (x + 1) * lanes)
            field = field_ref[first_tile + y, :, part]
            values = base_ref[t, 0:species, part]

            def add(values, axis, far, value):
                speed = field[axis : axis + 1]
                if far > 0:
                    speed = -speed
                return values + (speed * 8.0 + spread * 16.0 if abs(far) == 1 else -speed - spread) * value

            if first_x == 0:
                taps = ((-2, 0), (-1, 1)) if x == 0 else ((-2, 1),)
            else:
                taps = ((2, 0),) if x == 0 else ((1, 0), (2, 1))
            for far, plane in taps:
                values = add(values, 0, far, side(y, plane)[...])
            column = first_x + x
            if y == 0:
                values = add(values, 1, -2, ylo(0, column)[...])
            if y <= 1:
                values = add(values, 1, -1 - y, ylo(1, column)[...])
            if y >= depth - 2:
                values = add(values, 1, depth - y, yhi(0, column)[...])
            if y == depth - 1:
                values = add(values, 1, 2, yhi(1, column)[...])
            advected_ref[t, 0:species, part] = values
            current_ref[t, 0:species, part] = values
        current_ref[t, species:ROWS] = jnp.ones((ROWS - species, 2 * lanes), jnp.float32)

    row_ids = lax.broadcasted_iota(jnp.int32, (16, 2 * lanes), 0) + (ROWS - 16)
    is_species = row_ids < species
    is_one = (row_ids == species) | (row_ids == species + 2) | (row_ids == species + 3)
    is_heat = (row_ids == species + 1) | (row_ids == species + 4) | (row_ids == species + 5)

    def exponent(t):
        logged = jnp.log(jnp.maximum(current_ref[t], CONC_FLOOR)) * LOG2E
        spare = jnp.where(is_one, 1.0, jnp.where(is_heat, field_ref[first_tile + rows[t], 3:4], 0.0))
        stacked = jnp.concatenate(
            [logged[: ROWS - 16], jnp.where(is_species, logged[ROWS - 16 :], spare)], axis=0
        )
        return jnp.dot(gather_ref[...], split(stacked), preferred_element_type=jnp.float32)

    def gained(powers):
        total = None
        for j, (start, size) in enumerate(chunks(powers.shape[0])):
            progress = jnp.exp2(jnp.minimum(powers[start : start + size], LOG2E))
            part = jnp.dot(
                change_ref[j, :, 0 : 2 * size], split(progress), preferred_element_type=jnp.float32
            )
            total = part if total is None else total + part
        return CHEM_DT * total

    def settled(t):
        y = rows[t]
        picked = []
        for x in range(2):
            part = slice(x * lanes, (x + 1) * lanes)
            reacts = field_ref[first_tile + y, 4:5, part] > 0.5
            picked.append(jnp.where(reacts, current_ref[t, 0:species, part], advected_ref[t, :, part]))
        return picked

    copies = []
    if first_x == 0:
        write = strided(whole_ref)
        others = [middle_ref.at[y - 2] if 2 <= y < depth - 2 else edge_ref.at[y if y < 2 else y - depth + 4] for y in rows]
        for y in rows:
            for x in range(2):
                write(y, x + 2)[...] = others[y][0:species, x * lanes : (x + 1) * lanes]

    order = [(i, t) for i in range(SUBSTEPS) for t in range(tiles)]
    ready = exponent(0)
    for n, (i, t) in enumerate(order):
        powers = ready
        if n + 1 < len(order):
            ready = exponent(order[n + 1][1])
        current_ref[t] = current_ref[t] + gained(powers)
        if i + 1 < SUBSTEPS:
            continue
        picked = settled(t)
        for x in range(2):
            if first_x == 0:
                write(rows[t], x)[...] = picked[x]
            else:
                out_ref[t, 0:species, x * lanes : (x + 1) * lanes] = picked[x]
        if first_x == 0:
            y = rows[t]
            copies.append(pltpu.make_async_copy(whole_ref.at[:, y], out_ref.at[:, y], sems.at[t]))
            copies[-1].start()
    for copy in copies:
        copy.wait()


def part(first_x, rows, shape, *args):
    species, _, _, lanes = shape
    tiles = len(rows)
    block = (tiles, ROWS, 2 * lanes)
    scratch = [
        pltpu.VMEM((tiles, species, 2 * lanes), jnp.float32),
        pltpu.VMEM(block, jnp.float32),
    ]
    if first_x == 0:
        scratch += [pltpu.VMEM(shape, jnp.float32), pltpu.SemaphoreType.DMA((tiles,))]
    return pl.pallas_call(
        functools.partial(part_kernel, first_x, rows),
        out_shape=pltpu.VMEM(block, jnp.float32) if first_x else jax.ShapeDtypeStruct(shape, jnp.float32),
        out_specs=pl.BlockSpec() if first_x else pl.BlockSpec(memory_space=pl.ANY),
        scratch_shapes=scratch,
        compiler_params=pltpu.CompilerParams(vmem_limit_bytes=VMEM_LIMIT),
    )(*args)


def per_device(
    molar_fractions,
    fluid_speed_vector,
    thermal_state,
    molecular_spreading,
    arrhenius_ln_amplitude,
    arrhenius_energy,
    consumed_molecules,
    resulting_molecules,
    patch_assignee,
):
    species, _, depth, _ = molar_fractions.shape
    cells = molar_fractions.transpose(0, 2, 1, 3)
    flow_next, flow_back = ring("flow")
    chem_next, chem_back = ring("chem")
    xlo = lax.ppermute(jax.lax.optimization_barrier(last_planes(cells)), "flow", flow_next)
    again = lax.optimization_barrier(cells)
    xhi = lax.ppermute(again[:, :, :2], "flow", flow_back)
    ylo = lax.ppermute(cells[:, depth - 2 :], "chem", chem_next)
    yhi = lax.ppermute(cells[:, :2], "chem", chem_back)

    workers = lax.axis_size("chem")
    place = lax.axis_index("chem").astype(jnp.int32).reshape(1)
    gather, change, field, spread, lower, middle, edge = prepare(
        workers,
        place,
        patch_assignee,
        cells,
        fluid_speed_vector.transpose(0, 2, 1, 3),
        thermal_state.transpose(1, 0, 2),
        molecular_spreading.reshape(1, species),
        arrhenius_ln_amplitude.reshape(1, -1),
        arrhenius_energy.reshape(1, -1),
        consumed_molecules.T,
        resulting_molecules.T,
    )
    shared = tuple(map(on_chip, (field, spread, gather, change)))
    xlo, xhi, ylo, yhi, lower, middle, edge = map(on_chip, (xlo, xhi, ylo, yhi, lower, middle, edge))
    inner = tuple(range(2, depth - 2))
    outer = (0, 1, depth - 2, depth - 1)
    middle = part(2, inner, cells.shape, middle, xhi, xhi, xhi, *shared)
    edge = part(2, outer, cells.shape, edge, xhi, ylo, yhi, *shared)
    out = part(
        0, tuple(range(depth)), cells.shape, lower, xlo, ylo, yhi, *shared,
        on_chip(middle), on_chip(edge)
    )
    return out.transpose(0, 2, 1, 3)


def solution(mesh):
    in_specs = (
        P(None, "flow", "chem", None),
        P(None, "flow", "chem", None),
        P("flow", "chem", None),
        P(),
        P(),
        P(),
        P(),
        P(),
        P("flow", None),
    )
    out_specs = P(None, "flow", "chem", None)
    return jax.shard_map(
        per_device, mesh=mesh, in_specs=in_specs, out_specs=out_specs, check_vma=False
    )
```

```python
import functools

import jax
import jax.numpy as jnp
from jax import lax
from jax.experimental import pallas as pl
from jax.experimental.pallas import tpu as pltpu
from jax.sharding import PartitionSpec as P

PATCHES_ON_UNIT = 14
SUBSTEPS = 4
LOG2E = 1.4426950408889634
CONC_FLOOR = 0.1
CHEM_DT = 0.04
ROWS = 64
CHUNK = 128
VMEM_LIMIT = 12 << 20


def ring(axis):
    count = lax.axis_size(axis)
    forward = [(i, (i + 1) % count) for i in range(count)]
    return forward, [(target, source) for source, target in forward]


def on_chip(values):
    return pltpu.with_memory_space_constraint(values, pltpu.VMEM)


def chunks(count):
    padded = -(-count // 16) * 16
    return [(start, min(CHUNK, padded - start)) for start in range(0, padded, CHUNK)]


def split(values):
    high = values.astype(jnp.bfloat16)
    low = (values - high.astype(jnp.float32)).astype(jnp.bfloat16)
    return jnp.concatenate([high, low], axis=0)


def pieces(values):
    high = values.astype(jnp.bfloat16).astype(jnp.float32)
    middle = (values - high).astype(jnp.bfloat16).astype(jnp.float32)
    return high, middle, values - high - middle


def strided(ref):
    species, ys, xs, lanes = ref.shape
    flat = ref.reshape(species * ys * xs, lanes)
    return lambda y, x: flat.at[pl.ds(y * xs + x, species, stride=ys * xs), :]


def cut_kernel(cells_ref, out_ref, sem):
    copy = pltpu.make_async_copy(cells_ref.at[:, :, cells_ref.shape[2] - 2 :], out_ref, sem)
    copy.start()
    copy.wait()


def last_planes(cells):
    species, depth, _, lanes = cells.shape
    return pl.pallas_call(
        cut_kernel,
        out_shape=pltpu.VMEM((species, depth, 2, lanes), jnp.float32),
        in_specs=[pl.BlockSpec(memory_space=pltpu.HBM)],
        scratch_shapes=[pltpu.SemaphoreType.DMA],
        compiler_params=pltpu.CompilerParams(vmem_limit_bytes=VMEM_LIMIT),
        name="cut",
    )(pltpu.with_memory_space_constraint(cells, pltpu.HBM))


def prepare_kernel(
    workers, place_ref, owner_ref, u_ref, speed_ref, heat_ref, spread_ref, amplitude_ref, energy_ref, consumed_ref, resulting_ref,
    gather_ref, change_ref, field_ref, slow_ref, lower_ref, middle_ref, edge_ref, wide_ref, index_ref, rate_ref
):
    species, depth, width, lanes = u_ref.shape
    count = consumed_ref.shape[1]
    reach = index_ref.shape[1]
    slab = wide_ref.shape[1]
    stride = depth + 4

    index_ref[...] = jnp.full(index_ref.shape, -1, jnp.int32)
    index_ref[0:2, 0:count] = consumed_ref[...]
    index_ref[2:4, 0:count] = resulting_ref[...]
    rate_ref[...] = jnp.zeros_like(rate_ref)
    rate_ref[0:1, 0:count] = amplitude_ref[...] * LOG2E
    rate_ref[1:2, 0:count] = energy_ref[...] * -LOG2E
    ids = lax.broadcasted_iota(jnp.int32, (ROWS, reach), 0)
    ones = [jnp.where(index_ref[k : k + 1] == ids, 1.0, 0.0) for k in range(4)]
    used = ones[0] + ones[1]
    change = ones[2] + ones[3] - used
    a_high, a_middle, a_low = pieces(rate_ref[0:1])
    e_high, e_middle, e_low = pieces(rate_ref[1:2])
    for k, row in enumerate((a_high, e_high, a_middle, a_low, e_middle, e_low)):
        used = jnp.where(ids == species + k, row, used)
    both = jnp.concatenate([used, used], axis=0)
    rows = gather_ref.shape[0]
    for start in range(0, reach, lanes):
        size = min(lanes, rows - start)
        part = jnp.transpose(both[:, start : start + lanes])
        gather_ref[start : start + size] = part[0:size].astype(jnp.bfloat16)
    lane = lax.broadcasted_iota(jnp.int32, (ROWS, 2 * CHUNK), 1)
    for j, (start, size) in enumerate(chunks(count)):
        part = change[:, start : start + CHUNK]
        pair = jnp.concatenate([part, jnp.zeros_like(part)], axis=1)
        pair = jnp.where(lane < size, pair, 0.0)
        change_ref[j] = (pair + pltpu.roll(pair, size, 1)).astype(jnp.bfloat16)

    for x in range(width):
        for y in range(depth):
            t, k = x // 2 * depth + y, x % 2
            part = slice(k * lanes, (k + 1) * lanes)
            for c in range(3):
                field_ref[t, c : c + 1, part] = speed_ref[c, y, x : x + 1, :] * (1.0 / 12.0)
            field_ref[t, 3:4, part] = 1.0 / heat_ref[y, x : x + 1, :]
            block = place_ref[0] * PATCHES_ON_UNIT + (x * depth + y) // 2
            reacts = jnp.where(owner_ref[0, block] < workers, 1.0, 0.0)
            field_ref[t, 4:5, part] = jnp.full((1, lanes), reacts, jnp.float32)
    spread = jnp.concatenate([spread_ref[...], jnp.zeros((1, lanes - species), jnp.float32)], axis=1)
    spread = jnp.transpose(jnp.broadcast_to(spread * (1.0 / 12.0), (lanes, lanes)))[0:slab]
    slow_ref[...] = spread

    for slot in range(width + 4):
        for y in range(stride):
            if 2 <= slot < width + 2 and 2 <= y < depth + 2:
                wide_ref[slot * stride + y, 0:species, :] = strided(u_ref)(y - 2, slot - 2)[...]
            elif 2 <= slot < width + 2 or 2 <= y < depth + 2:
                wide_ref[slot * stride + y] = jnp.zeros((slab, lanes), jnp.float32)

    def advect(x, y, field):
        base = (x + 2) * stride + y + 2
        center = wide_ref[base]
        near = jnp.zeros_like(center)
        far = jnp.zeros_like(center)
        moved = jnp.zeros_like(center)
        for axis in range(3):
            if axis == 2:
                low2 = pltpu.roll(center, 2, 1)
                low1 = pltpu.roll(center, 1, 1)
                high1 = pltpu.roll(center, lanes - 1, 1)
                high2 = pltpu.roll(center, lanes - 2, 1)
            else:
                hop = stride if axis == 0 else 1
                low2 = wide_ref[base - 2 * hop]
                low1 = wide_ref[base - hop]
                high1 = wide_ref[base + hop]
                high2 = wide_ref[base + 2 * hop]
            moved = moved + field[axis : axis + 1] * (8.0 * (high1 - low1) - (high2 - low2))
            near = near + (high1 + low1)
            far = far + (high2 + low2)
        return center - moved + spread * (16.0 * near - far - 90.0 * center)

    skipped = middle_ref.shape[0]
    first = edge_ref.shape[0] // 2
    for target, x0, row in (
        (lower_ref, 0, lambda t: t),
        (middle_ref, 2, lambda t: t + first),
        (edge_ref, 2, lambda t: t + jnp.where(t >= first, skipped, 0)),
    ):
        def tile(t, carry, target=target, x0=x0, row=row):
            y = row(t)
            for k in range(2):
                part = slice(k * lanes, (k + 1) * lanes)
                target[t, 0:slab, part] = advect(x0 + k, y, field_ref[x0 // 2 * depth + y, :, part])
            target[t, slab:ROWS] = jnp.zeros((ROWS - slab, 2 * lanes), jnp.float32)
            return carry

        lax.fori_loop(0, target.shape[0], tile, 0)


def prepare(workers, place, owners, cells, *args):
    consumed = args[-1]
    species, depth, width, lanes = cells.shape
    count = consumed.shape[1]
    parts = chunks(count)
    reach = len(parts) * CHUNK
    slab = -(-species // 8) * 8
    tiles = width * depth // 2
    shapes = [
        ((parts[-1][0] + parts[-1][1], 2 * ROWS), jnp.bfloat16),
        ((len(parts), ROWS, 2 * CHUNK), jnp.bfloat16),
        ((tiles, 8, 2 * lanes), jnp.float32),
        ((slab, lanes), jnp.float32),
        ((depth, ROWS, 2 * lanes), jnp.float32),
        ((depth - 4, ROWS, 2 * lanes), jnp.float32),
        ((4, ROWS, 2 * lanes), jnp.float32),
    ]
    return pl.pallas_call(
        functools.partial(prepare_kernel, workers),
        out_shape=[pltpu.VMEM(*shape) for shape in shapes],
        in_specs=[pl.BlockSpec(memory_space=pltpu.SMEM)] * 2 + [pl.BlockSpec()] * (1 + len(args)),
        scratch_shapes=[
            pltpu.VMEM(((width + 4) * (depth + 4), slab, lanes), jnp.float32),
            pltpu.VMEM((8, reach), jnp.int32),
            pltpu.VMEM((8, reach), jnp.float32),
        ],
        compiler_params=pltpu.CompilerParams(vmem_limit_bytes=VMEM_LIMIT),
        name="prepare",
    )(place, owners, cells, *args)


def part_kernel(first_x, rows, *refs):
    base_ref, side_ref, ylo_ref, yhi_ref, field_ref, spread_ref, gather_ref, change_ref = refs[:8]
    if first_x == 0:
        middle_ref, edge_ref, out_ref, advected_ref, current_ref, whole_ref, sems = refs[8:]
    else:
        out_ref, advected_ref, current_ref = refs[8:]
    species, depth, _, lanes = side_ref.shape
    tiles = len(rows)
    first_tile = first_x // 2 * depth
    side, ylo, yhi = strided(side_ref), strided(ylo_ref), strided(yhi_ref)
    spread = spread_ref[0:species]

    for t, y in enumerate(rows):
        for x in range(2):
            part = slice(x * lanes, (x + 1) * lanes)
            field = field_ref[first_tile + y, :, part]
            values = base_ref[t, 0:species, part]

            def add(values, axis, far, value):
                speed = field[axis : axis + 1]
                if far > 0:
                    speed = -speed
                return values + (speed * 8.0 + spread * 16.0 if abs(far) == 1 else -speed - spread) * value

            if first_x == 0:
                taps = ((-2, 0), (-1, 1)) if x == 0 else ((-2, 1),)
            else:
                taps = ((2, 0),) if x == 0 else ((1, 0), (2, 1))
            for far, plane in taps:
                values = add(values, 0, far, side(y, plane)[...])
            column = first_x + x
            if y == 0:
                values = add(values, 1, -2, ylo(0, column)[...])
            if y <= 1:
                values = add(values, 1, -1 - y, ylo(1, column)[...])
            if y >= depth - 2:
                values = add(values, 1, depth - y, yhi(0, column)[...])
            if y == depth - 1:
                values = add(values, 1, 2, yhi(1, column)[...])
            advected_ref[t, 0:species, part] = values
            current_ref[t, 0:species, part] = values
        current_ref[t, species:ROWS] = jnp.ones((ROWS - species, 2 * lanes), jnp.float32)

    row_ids = lax.broadcasted_iota(jnp.int32, (16, 2 * lanes), 0) + (ROWS - 16)
    is_species = row_ids < species
    is_one = (row_ids == species) | (row_ids == species + 2) | (row_ids == species + 3)
    is_heat = (row_ids == species + 1) | (row_ids == species + 4) | (row_ids == species + 5)

    def exponent(t):
        logged = jnp.log(jnp.maximum(current_ref[t], CONC_FLOOR)) * LOG2E
        spare = jnp.where(is_one, 1.0, jnp.where(is_heat, field_ref[first_tile + rows[t], 3:4], 0.0))
        stacked = jnp.concatenate(
            [logged[: ROWS - 16], jnp.where(is_species, logged[ROWS - 16 :], spare)], axis=0
        )
        return jnp.dot(gather_ref[...], split(stacked), preferred_element_type=jnp.float32)

    def gained(powers):
        total = None
        for j, (start, size) in enumerate(chunks(powers.shape[0])):
            progress = jnp.exp2(jnp.minimum(powers[start : start + size], LOG2E))
            part = jnp.dot(
                change_ref[j, :, 0 : 2 * size], split(progress), preferred_element_type=jnp.float32
            )
            total = part if total is None else total + part
        return CHEM_DT * total

    def settled(t):
        y = rows[t]
        picked = []
        for x in range(2):
            part = slice(x * lanes, (x + 1) * lanes)
            reacts = field_ref[first_tile + y, 4:5, part] > 0.5
            picked.append(jnp.where(reacts, current_ref[t, 0:species, part], advected_ref[t, :, part]))
        return picked

    copies = []
    if first_x == 0:
        write = strided(whole_ref)
        others = [middle_ref.at[y - 2] if 2 <= y < depth - 2 else edge_ref.at[y if y < 2 else y - depth + 4] for y in rows]
        for y in rows:
            for x in range(2):
                write(y, x + 2)[...] = others[y][0:species, x * lanes : (x + 1) * lanes]

    order = [(i, t) for i in range(SUBSTEPS) for t in range(tiles)]
    for i, t in order:
        powers = exponent(t)
        current_ref[t] = current_ref[t] + gained(powers)
        if i + 1 < SUBSTEPS:
            continue
        picked = settled(t)
        for x in range(2):
            if first_x == 0:
                write(rows[t], x)[...] = picked[x]
            else:
                out_ref[t, 0:species, x * lanes : (x + 1) * lanes] = picked[x]
        if first_x == 0:
            y = rows[t]
            copies.append(pltpu.make_async_copy(whole_ref.at[:, y], out_ref.at[:, y], sems.at[t]))
            copies[-1].start()
    for copy in copies:
        copy.wait()


def part(first_x, rows, shape, *args):
    species, _, _, lanes = shape
    tiles = len(rows)
    block = (tiles, ROWS, 2 * lanes)
    scratch = [
        pltpu.VMEM((tiles, species, 2 * lanes), jnp.float32),
        pltpu.VMEM(block, jnp.float32),
    ]
    if first_x == 0:
        scratch += [pltpu.VMEM(shape, jnp.float32), pltpu.SemaphoreType.DMA((tiles,))]
    return pl.pallas_call(
        functools.partial(part_kernel, first_x, rows),
        out_shape=pltpu.VMEM(block, jnp.float32) if first_x else jax.ShapeDtypeStruct(shape, jnp.float32),
        out_specs=pl.BlockSpec() if first_x else pl.BlockSpec(memory_space=pl.ANY),
        scratch_shapes=scratch,
        compiler_params=pltpu.CompilerParams(vmem_limit_bytes=VMEM_LIMIT),
    )(*args)


def per_device(
    molar_fractions,
    fluid_speed_vector,
    thermal_state,
    molecular_spreading,
    arrhenius_ln_amplitude,
    arrhenius_energy,
    consumed_molecules,
    resulting_molecules,
    patch_assignee,
):
    species, _, depth, _ = molar_fractions.shape
    cells = molar_fractions.transpose(0, 2, 1, 3)
    flow_next, flow_back = ring("flow")
    chem_next, chem_back = ring("chem")
    xlo = lax.ppermute(jax.lax.optimization_barrier(last_planes(cells)), "flow", flow_next)
    again = lax.optimization_barrier(cells)
    xhi = lax.ppermute(again[:, :, :2], "flow", flow_back)
    ylo = lax.ppermute(cells[:, depth - 2 :], "chem", chem_next)
    yhi = lax.ppermute(cells[:, :2], "chem", chem_back)

    workers = lax.axis_size("chem")
    place = lax.axis_index("chem").astype(jnp.int32).reshape(1)
    gather, change, field, spread, lower, middle, edge = prepare(
        workers,
        place,
        patch_assignee,
        cells,
        fluid_speed_vector.transpose(0, 2, 1, 3),
        thermal_state.transpose(1, 0, 2),
        molecular_spreading.reshape(1, species),
        arrhenius_ln_amplitude.reshape(1, -1),
        arrhenius_energy.reshape(1, -1),
        consumed_molecules.T,
        resulting_molecules.T,
    )
    shared = tuple(map(on_chip, (field, spread, gather, change)))
    xlo, xhi, ylo, yhi, lower, middle, edge = map(on_chip, (xlo, xhi, ylo, yhi, lower, middle, edge))
    inner = tuple(range(2, depth - 2))
    outer = (0, 1, depth - 2, depth - 1)
    middle = part(2, inner, cells.shape, middle, xhi, xhi, xhi, *shared)
    edge = part(2, outer, cells.shape, edge, xhi, ylo, yhi, *shared)
    out = part(
        0, tuple(range(depth)), cells.shape, lower, xlo, ylo, yhi, *shared,
        on_chip(middle), on_chip(edge)
    )
    return out.transpose(0, 2, 1, 3)


def solution(mesh):
    in_specs = (
        P(None, "flow", "chem", None),
        P(None, "flow", "chem", None),
        P("flow", "chem", None),
        P(),
        P(),
        P(),
        P(),
        P(),
        P("flow", None),
    )
    out_specs = P(None, "flow", "chem", None)
    return jax.shard_map(
        per_device, mesh=mesh, in_specs=in_specs, out_specs=out_specs, check_vma=False
    )
```
